128 devices in a mesh: lane: 64 (over z, y, x), ctx: 2 (over core).
Axes of the slice: x: 4, y: 4, z: 4, core: 2. Of those that a mesh axis runs over, the one named last changes fastest.
Arguments:
- view_tokens: bfloat16 [64, 2048, 768], P('lane', 'ctx'), may hold values from -6 to 6
- destinations: int32 [64, 128], P('lane', 'ctx'), may hold values from 0 to 63, as said below
- w_query: bfloat16 [768, 768], replicated, may hold values from -0.21875 to 0.21875
- w_key: bfloat16 [768, 768], replicated, may hold values from -0.21875 to 0.21875
- w_value: bfloat16 [768, 768], replicated, may hold values from -0.21875 to 0.21875
- rate_vector: bfloat16 [768], replicated, may hold values from -0.21875 to 0.21875
- fast_gate: bfloat16 [768, 768], replicated, may hold values from -0.21875 to 0.21875
- fast_up: bfloat16 [768, 768], replicated, may hold values from -0.21875 to 0.21875
- fast_down: bfloat16 [768, 768], replicated, may hold values from -0.21875 to 0.21875
- out_gain: float32 [768], replicated, may hold values from 0.1 to 1.9
Outputs:
- ttt_output: bfloat16 [64, 2048, 768], P('lane', 'ctx')
The draws below stay inside these ranges and needn't reach their ends.
Inputs may be any that keep to these rules, and one draw needn't show every extreme that they name: `destinations`: for every source device and every segment, the 64 entries name every lane once, except that one lane is named twice and one lane not at all; over all source devices of one segment every lane is named exactly 64 times.
All inputs are finite; a program needn't handle non-finite values.
Results may differ from the reference program's by a relative error of at most 0.012.
Values may be sent and summed in bfloat16 or wider, within the bound.
A program may use at most 128 MiB of HBM per device.

```python
import jax
import jax.numpy as jnp
from jax import lax

D = 768
SEGMENT = 1024
SCENES = 1
LANES = 64
CTX = 2
BLK = 16


def draw_destinations(key, part):

    def one_context(ctx_key):
        key_perm, key_shift, key_rows = jax.random.split(ctx_key, 3)
        mapping = jax.random.permutation(key_perm, LANES)
        shift_by = jax.random.randint(key_shift, (), 1, LANES)
        sources = jnp.arange(LANES)
        dropped = mapping[(sources + shift_by) % LANES]
        lane_row = jnp.arange(LANES)[None, :]
        base_rows = jnp.where(lane_row == dropped[:, None], mapping[:, None], lane_row)
        row_keys = jax.random.split(key_rows, LANES)
        return jax.vmap(lambda row_key, entries: jax.random.permutation(row_key, entries))(row_keys, base_rows)
    per_context = jax.vmap(one_context)(jax.random.split(jax.random.fold_in(key, 17), CTX))
    return per_context.transpose(1, 0, 2).reshape(LANES, CTX * LANES).astype(jnp.int32)


def steps_of(rng, shape, pieces, low, high):
    loudness, own = 1.0, jax.random.fold_in(rng, 6)
    for axis_at, shards_of in pieces:
        steps = jnp.exp(jax.random.uniform(jax.random.fold_in(own, axis_at), (shards_of,), jnp.float32, low / len(pieces), high / len(pieces)))
        loudness = loudness * jnp.repeat(steps, shape[axis_at] // shards_of).reshape([-1 if axis == axis_at else 1 for axis in range(len(shape))])
    return loudness


def scatter_about(stream_key, shape, spread, limit, pieces=(), kind=jnp.bfloat16):
    drawn = spread * jax.random.normal(stream_key, shape, jnp.float32)
    if pieces:
        drawn = drawn * steps_of(stream_key, shape, pieces, -0.22, 0.18)
    return jnp.clip(drawn, -limit, limit).astype(kind)


def setup_inputs(seed: int = 0) -> dict:
    keys = jax.random.split(jax.random.key(seed), 11)
    return {
        "view_tokens": scatter_about(keys[0], (LANES, CTX * SCENES * SEGMENT, D), 1.0, 6.0, ((0, 64), (1, 2))),
        "destinations": draw_destinations(jax.random.fold_in(keys[10], 71), 0),
        "w_query": scatter_about(keys[2], (D, D), D ** -0.5, 0.21875),
        "w_key": scatter_about(keys[3], (D, D), D ** -0.5, 0.21875),
        "w_value": scatter_about(keys[4], (D, D), D ** -0.5, 0.21875),
        "rate_vector": scatter_about(keys[5], (D,), D ** -0.5, 0.21875),
        "fast_gate": scatter_about(keys[6], (D, D), D ** -0.5, 0.21875),
        "fast_up": scatter_about(keys[7], (D, D), D ** -0.5, 0.21875),
        "fast_down": scatter_about(keys[8], (D, D), D ** -0.5, 0.21875),
        "out_gain": jnp.clip(1.0 + 0.18 * jax.random.normal(keys[9], (D,), jnp.float32), 0.1, 1.9),
    }


def row_scale(values):
    return lax.rsqrt(lax.optimization_barrier(jnp.mean(values * values, axis=-1, keepdims=True)) + 1e-06)

def dot_f32(left_side, right_side):
    return jnp.dot(left_side, right_side, preferred_element_type=jnp.float32)

def contract_rows(left_side, right_side):
    return lax.dot_general(left_side, right_side, (((0,), (0,)), ((), ())), preferred_element_type=jnp.float32)

def project_tokens(tokens, w_query, w_key, w_value, rate_vector):
    query_pre = dot_f32(tokens, w_query)
    key_pre = dot_f32(tokens, w_key)
    queries_bf = (query_pre * row_scale(query_pre)).astype(jnp.bfloat16)
    keys_bf = (key_pre * row_scale(key_pre)).astype(jnp.bfloat16)
    token_rates = jax.nn.softplus(dot_f32(tokens, rate_vector))
    scaled_values = (token_rates[:, None] * dot_f32(tokens, w_value)).astype(jnp.bfloat16)
    return (queries_bf, keys_bf, scaled_values)

def fast_update(gate_w, up_w, down_w, keys_bf, scaled_values):
    gate_pre = dot_f32(keys_bf, gate_w)
    up_pre = dot_f32(keys_bf, up_w)
    gate_sig = jax.nn.sigmoid(gate_pre)
    hidden = (gate_pre * gate_sig * up_pre).astype(jnp.bfloat16)
    back = lax.dot_general(scaled_values, down_w, (((1,), (1,)), ((), ())), preferred_element_type=jnp.float32)
    gate_term = (back * up_pre * gate_sig * (1.0 + gate_pre * (1.0 - gate_sig))).astype(jnp.bfloat16)
    up_term = (back * gate_pre * gate_sig).astype(jnp.bfloat16)
    gradients = (contract_rows(keys_bf, gate_term), contract_rows(keys_bf, up_term), contract_rows(hidden, scaled_values))
    step_size = 0.5 * gate_w.shape[0] ** (-0.5)
    renewed = []
    for previous, gradient in zip((gate_w, up_w, down_w), gradients):
        renewed.append((previous.astype(jnp.float32) + step_size * gradient * row_scale(gradient)).astype(jnp.bfloat16))
    return tuple(renewed)

def apply_queries(gate_w, up_w, down_w, queries_bf, out_gain):
    q_gate = dot_f32(queries_bf, gate_w)
    q_up = dot_f32(queries_bf, up_w)
    q_hidden = (jax.nn.silu(q_gate) * q_up).astype(jnp.bfloat16)
    output_pre = dot_f32(q_hidden, down_w)
    return (output_pre * row_scale(output_pre) * out_gain).astype(jnp.bfloat16)

def reference(view_tokens, destinations, w_query, w_key, w_value, rate_vector, fast_gate, fast_up, fast_down, out_gain):
    blocks = view_tokens.reshape(LANES, CTX, LANES, BLK, D)
    routes = destinations.reshape(LANES, CTX, LANES)
    source_order = jnp.arange(LANES * LANES, dtype=jnp.int32)
    routed = []
    for ctx_index in range(CTX):
        chosen = routes[:, ctx_index, :]
        sort_keys = chosen.reshape(-1) * (LANES * LANES) + source_order
        ordering = jnp.argsort(sort_keys)
        flat_blocks = blocks[:, ctx_index].reshape(LANES * LANES, BLK * D)
        routed.append(flat_blocks[ordering].reshape(LANES, SCENES, SEGMENT, D))
    routed = jnp.stack(routed)
    scenes = routed.transpose(1, 2, 0, 3, 4).reshape(SCENES * LANES, CTX, SEGMENT, D)

    def run_scene(scene_tokens):
        weights = (fast_gate, fast_up, fast_down)
        outputs = []
        for ctx_index in range(CTX):
            queries_bf, keys_bf, scaled_values = project_tokens(scene_tokens[ctx_index], w_query, w_key, w_value, rate_vector)
            weights = fast_update(weights[0], weights[1], weights[2], keys_bf, scaled_values)
            outputs.append(apply_queries(weights[0], weights[1], weights[2], queries_bf, out_gain))
        return jnp.concatenate(outputs, axis=0)
    return lax.map(run_scene, scenes)
```

```python
import functools

import jax
import jax.numpy as jnp
from jax import lax
from jax.experimental import pallas as pl
from jax.experimental.pallas import tpu as pltpu
from jax.sharding import PartitionSpec as P

MESH = pl.DeviceIdType.MESH
LANES = 64
BLK = 16
SIDE = 4
ORDERS = ((2, 1, 0), (0, 2, 1), (1, 0, 2))


def coords_of(lane):
    return (lane // 16, (lane // 4) % 4, lane % 4)


def lane_of(coords):
    return coords[0] * 16 + coords[1] * 4 + coords[2]


def route_kernel(idx_ref, meta_ref, view_ref, buf_ref, all_meta_ref, send, extra, send_sem, recv_sem,
                 ext_send, ext_recv, meta_send, meta_recv, local_sem):
    me = lax.axis_index("lane")
    ctx = lax.axis_index("ctx")
    here = coords_of(me)
    width = view_ref.shape[2]
    part = width // 3

    barrier = pltpu.get_barrier_semaphore()

    def greet(k, carry):
        pl.semaphore_signal(barrier, inc=1, device_id=(lax.rem(me + k, LANES), ctx), device_id_type=MESH)
        return carry

    lax.fori_loop(1, LANES, greet, 0)

    extra[...] = view_ref[idx_ref[LANES]]

    def peer(offset):
        d = coords_of(offset)
        return lane_of([(h + o) % SIDE for h, o in zip(here, d)])

    def pack(k, carry):
        offset = lax.rem(k * 21, LANES)
        send[offset] = view_ref[idx_ref[peer(offset)]]
        return carry

    lax.fori_loop(0, LANES, pack, 0)
    pl.semaphore_wait(barrier, LANES - 1)

    own_extra = pltpu.make_async_copy(extra, buf_ref.at[1, here[0], here[1], here[2]], local_sem.at[0])
    own_prim = pltpu.make_async_copy(send.at[0], buf_ref.at[0, 0, 0, 0], local_sem.at[1])
    own_meta = pltpu.make_async_copy(meta_ref, all_meta_ref.at[here[0], here[1], here[2]], local_sem.at[2])
    own_extra.start()
    own_prim.start()
    own_meta.start()

    def held(p, stage, coords):
        done = ORDERS[p][:stage]
        spot = [pl.ds(0, SIDE) if a in done else coords[a] for a in range(3)]
        return spot

    def ext_copy(p, stage, delta, back):
        axis = ORDERS[p][stage]
        coords = list(here)
        if back:
            coords[axis] = (here[axis] - delta) % SIDE
        z, y, x = held(p, stage, coords)
        slab = buf_ref.at[1, z, y, x, :, pl.ds(p * part, part)]
        source = extra.at[:, pl.ds(p * part, part)] if stage == 0 else slab
        if back:
            source = slab
        to = list(here)
        to[axis] = (here[axis] + delta) % SIDE
        return pltpu.make_async_remote_copy(
            src_ref=source, dst_ref=slab,
            send_sem=ext_send.at[p, stage, delta - 1], recv_sem=ext_recv.at[p, stage, delta - 1],
            device_id=(lane_of(to), ctx), device_id_type=MESH)

    def meta_copy(stage, delta, back):
        axis = ORDERS[0][stage]
        coords = list(here)
        if back:
            coords[axis] = (here[axis] - delta) % SIDE
        z, y, x = held(0, stage, coords)
        slab = all_meta_ref.at[z, y, x]
        to = list(here)
        to[axis] = (here[axis] + delta) % SIDE
        source = meta_ref if stage == 0 and not back else slab
        return pltpu.make_async_remote_copy(
            src_ref=source, dst_ref=slab,
            send_sem=meta_send.at[stage, delta - 1], recv_sem=meta_recv.at[stage, delta - 1],
            device_id=(lane_of(to), ctx), device_id_type=MESH)

    def start_stage(stage):
        for delta in (1, 3, 2):
            meta_copy(stage, delta, False).start()
            for p in range(3):
                ext_copy(p, stage, delta, False).start()

    def end_stage(stage):
        for delta in (1, 3, 2):
            meta_copy(stage, delta, True).wait_recv()
            for p in range(3):
                ext_copy(p, stage, delta, True).wait_recv()

    def post(k, carry):
        offset = lax.rem(k * 21, LANES)
        d = coords_of(offset)
        pltpu.make_async_remote_copy(
            src_ref=send.at[offset], dst_ref=buf_ref.at[0, d[0], d[1], d[2]],
            send_sem=send_sem, recv_sem=recv_sem,
            device_id=(peer(offset), ctx), device_id_type=MESH).start()
        return carry

    start_stage(0)
    lax.fori_loop(1, 22, post, 0)
    own_extra.wait()
    own_meta.wait()
    end_stage(0)
    start_stage(1)
    lax.fori_loop(22, 43, post, 0)
    end_stage(1)
    start_stage(2)
    lax.fori_loop(43, LANES, post, 0)
    end_stage(2)
    own_prim.wait()
    for stage in range(3):
        for delta in (1, 3, 2):
            meta_copy(stage, delta, False).wait_send()
            for p in range(3):
                ext_copy(p, stage, delta, False).wait_send()


    first = pltpu.make_async_remote_copy(
        src_ref=send.at[pl.ds(1, LANES - 1)], dst_ref=send.at[pl.ds(1, LANES - 1)],
        send_sem=send_sem, recv_sem=recv_sem,
        device_id=(peer(1), ctx), device_id_type=MESH)
    first.wait_send()
    first.wait_recv()


def route(idx, meta, blocks):
    width = blocks.shape[2]
    return pl.pallas_call(
        route_kernel,
        out_shape=(
            jax.ShapeDtypeStruct((2, SIDE, SIDE, SIDE, BLK, width), jnp.bfloat16),
            jax.ShapeDtypeStruct((SIDE, SIDE, SIDE, 1, 128), jnp.int32),
        ),
        in_specs=[
            pl.BlockSpec(memory_space=pltpu.SMEM),
            pl.BlockSpec(memory_space=pltpu.VMEM),
            pl.BlockSpec(memory_space=pltpu.VMEM),
        ],
        out_specs=(pl.BlockSpec(memory_space=pl.ANY), pl.BlockSpec(memory_space=pl.ANY)),
        scratch_shapes=[
            pltpu.VMEM((LANES, BLK, width), jnp.bfloat16),
            pltpu.VMEM((BLK, width), jnp.bfloat16),
            pltpu.SemaphoreType.DMA,
            pltpu.SemaphoreType.DMA,
            pltpu.SemaphoreType.DMA((3, 3, 3)),
            pltpu.SemaphoreType.DMA((3, 3, 3)),
            pltpu.SemaphoreType.DMA((3, 3)),
            pltpu.SemaphoreType.DMA((3, 3)),
            pltpu.SemaphoreType.DMA((3,)),
        ],
        compiler_params=pltpu.CompilerParams(
            collective_id=0, has_side_effects=True, vmem_limit_bytes=16 << 20
        ),
        name="route",
    )(idx, meta, blocks)


def project_kernel(meta_ref, buf_ref, wq_ref, wk_ref, wv_ref, rate_ref, q_ref, k_ref, v_ref, tokens, table, sems):
    me = lax.axis_index("lane")
    here = coords_of(me)

    def place(s, p):
        c = coords_of(s)
        slot = lane_of([(h - o) % SIDE for h, o in zip(here, c)])
        table[p] = slot
        p = p + (meta_ref[s, 1] != me).astype(jnp.int32)
        table[p] = s + LANES
        return p + (meta_ref[s, 0] == me).astype(jnp.int32)

    lax.fori_loop(0, LANES, place, jnp.int32(0))
    chunk_blocks = 16
    chunks = LANES // chunk_blocks

    def fetch(r, carry):
        pltpu.make_async_copy(buf_ref.at[table[r]], tokens.at[r], sems.at[r // chunk_blocks]).start()
        return carry

    lax.fori_loop(0, LANES, fetch, 0)

    def project(c, carry):
        span = pl.ds(c * chunk_blocks, chunk_blocks)
        pltpu.make_async_copy(buf_ref.at[span], tokens.at[span], sems.at[c]).wait()
        x = tokens[span].reshape(chunk_blocks * BLK, tokens.shape[2])
        rows = pl.ds(c * chunk_blocks * BLK, chunk_blocks * BLK)
        q = jnp.dot(x, wq_ref[...], preferred_element_type=jnp.float32)
        q_ref[rows, :] = (q * row_scale(q)).astype(jnp.bfloat16)
        k = jnp.dot(x, wk_ref[...], preferred_element_type=jnp.float32)
        k_ref[rows, :] = (k * row_scale(k)).astype(jnp.bfloat16)
        rate = jnp.dot(x, rate_ref[...], preferred_element_type=jnp.float32)
        rate = jnp.maximum(rate, 0.0) + jnp.log1p(jnp.exp(-jnp.abs(rate)))
        v = jnp.dot(x, wv_ref[...], preferred_element_type=jnp.float32)
        v_ref[rows, :] = (rate[:, :1] * v).astype(jnp.bfloat16)
        return carry

    lax.fori_loop(0, chunks, project, 0)


def row_scale(values):
    return lax.rsqrt(jnp.mean(values * values, axis=-1, keepdims=True) + 1e-06)


def project(meta, buf, w_query, w_key, w_value, rate):
    width = buf.shape[2]
    rows = LANES * BLK
    made = jax.ShapeDtypeStruct((rows, width), jnp.bfloat16)
    vmem = pl.BlockSpec(memory_space=pltpu.VMEM)
    return pl.pallas_call(
        project_kernel,
        out_shape=(made, made, made),
        in_specs=[pl.BlockSpec(memory_space=pltpu.SMEM), pl.BlockSpec(memory_space=pl.ANY), vmem, vmem, vmem, vmem],
        out_specs=(vmem, vmem, vmem),
        scratch_shapes=[
            pltpu.VMEM((LANES, BLK, width), jnp.bfloat16),
            pltpu.SMEM((LANES + 8,), jnp.int32),
            pltpu.SemaphoreType.DMA((4,)),
        ],
        compiler_params=pltpu.CompilerParams(vmem_limit_bytes=40 << 20),
        name="project",
    )(meta, buf, w_query, w_key, w_value, rate)


def dot_f32(left_side, right_side):
    return jnp.dot(left_side, right_side, preferred_element_type=jnp.float32)


def contract_rows(left_side, right_side):
    return lax.dot_general(
        left_side, right_side, (((0,), (0,)), ((), ())), preferred_element_type=jnp.float32
    )


def fast_update(gate_w, up_w, down_w, keys_bf, scaled_values):
    gate_pre = dot_f32(keys_bf, gate_w)
    up_pre = dot_f32(keys_bf, up_w)
    gate_sig = jax.nn.sigmoid(gate_pre)
    hidden = (gate_pre * gate_sig * up_pre).astype(jnp.bfloat16)
    back = lax.dot_general(
        scaled_values, down_w, (((1,), (1,)), ((), ())), preferred_element_type=jnp.float32
    )
    gate_term = (back * up_pre * gate_sig * (1.0 + gate_pre * (1.0 - gate_sig))).astype(
        jnp.bfloat16
    )
    up_term = (back * gate_pre * gate_sig).astype(jnp.bfloat16)
    gradients = (
        contract_rows(keys_bf, gate_term),
        contract_rows(keys_bf, up_term),
        contract_rows(hidden, scaled_values),
    )
    step_size = 0.5 * gate_w.shape[0] ** (-0.5)
    renewed = []
    for previous, gradient in zip((gate_w, up_w, down_w), gradients):
        renewed.append(
            (previous.astype(jnp.float32) + step_size * gradient * row_scale(gradient)).astype(
                jnp.bfloat16
            )
        )
    return tuple(renewed)


def apply_queries(gate_w, up_w, down_w, queries_bf, out_gain):
    q_gate = dot_f32(queries_bf, gate_w)
    q_up = dot_f32(queries_bf, up_w)
    q_hidden = (jax.nn.silu(q_gate) * q_up).astype(jnp.bfloat16)
    output_pre = dot_f32(q_hidden, down_w)
    return (output_pre * row_scale(output_pre) * out_gain).astype(jnp.bfloat16)


def body(
    view_tokens,
    destinations,
    w_query,
    w_key,
    w_value,
    rate_vector,
    fast_gate,
    fast_up,
    fast_down,
    out_gain,
):
    position = lax.axis_index("ctx")
    width = view_tokens.shape[2]
    blocks = view_tokens[0].reshape(LANES, BLK, width)
    lane_ids = jnp.arange(LANES, dtype=jnp.int32)
    named = destinations[0][:, None] == lane_ids[None, :]
    first = jnp.min(jnp.where(named, lane_ids[:, None], LANES), axis=0)
    last = jnp.max(jnp.where(named, lane_ids[:, None], -1), axis=0)
    twice = last > first
    extra = jnp.max(jnp.where(twice, last, -1))
    doubled = jnp.max(jnp.where(twice, lane_ids, -1))
    missed = jnp.max(jnp.where(first == LANES, lane_ids, -1))
    columns = jnp.arange(128, dtype=jnp.int32)
    idx = jnp.where(columns < LANES, jnp.pad(jnp.minimum(first, LANES - 1), (0, 64)), extra)
    meta = jnp.where(columns == 0, doubled, missed)[None, :]
    buf, all_meta = route(idx, meta, blocks)
    rate = jnp.broadcast_to(rate_vector[:, None], (width, 128))
    queries, keys, values = project(
        all_meta.reshape(LANES, 128), buf.reshape(2 * LANES, BLK, width), w_query, w_key, w_value, rate
    )
    initial = (fast_gate, fast_up, fast_down)
    updated = fast_update(*initial, keys, values)
    arrived = [lax.ppermute(w, "ctx", [(0, 1)]) for w in updated]
    weights = [jnp.where(position == 0, a, b) for a, b in zip(initial, arrived)]
    weights = fast_update(*weights, keys, values)
    return apply_queries(*weights, queries, out_gain)[None]


def solution(mesh):
    placed = (P("lane", "ctx", None), P("lane", "ctx"), P(), P(), P(), P(), P(), P(), P(), P())
    return jax.shard_map(
        body, mesh=mesh, in_specs=placed, out_specs=P("lane", "ctx", None), check_vma=False
    )
```

```python
import functools

import jax
import jax.numpy as jnp
from jax import lax
from jax.experimental import pallas as pl
from jax.experimental.pallas import tpu as pltpu
from jax.sharding import PartitionSpec as P

MESH = pl.DeviceIdType.MESH
LANES = 64
BLK = 16
SIDE = 4
ORDERS = ((2, 1, 0), (0, 2, 1), (1, 0, 2))


def coords_of(lane):
    return (lane // 16, (lane // 4) % 4, lane % 4)


def lane_of(coords):
    return coords[0] * 16 + coords[1] * 4 + coords[2]


def route_kernel(idx_ref, meta_ref, view_ref, buf_ref, all_meta_ref, send, extra, send_sem, recv_sem,
                 ext_send, ext_recv, meta_send, meta_recv, local_sem):
    me = lax.axis_index("lane")
    ctx = lax.axis_index("ctx")
    here = coords_of(me)
    width = view_ref.shape[2]
    part = width // 3

    barrier = pltpu.get_barrier_semaphore()

    def greet(k, carry):
        pl.semaphore_signal(barrier, inc=1, device_id=(lax.rem(me + k, LANES), ctx), device_id_type=MESH)
        return carry

    lax.fori_loop(1, LANES, greet, 0)

    extra[...] = view_ref[idx_ref[LANES]]

    def peer(offset):
        d = coords_of(offset)
        return lane_of([(h + o) % SIDE for h, o in zip(here, d)])

    def pack(k, carry):
        offset = lax.rem(k * 21, LANES)
        send[offset] = view_ref[idx_ref[peer(offset)]]
        return carry

    lax.fori_loop(0, LANES, pack, 0)
    pl.semaphore_wait(barrier, LANES - 1)

    own_extra = pltpu.make_async_copy(extra, buf_ref.at[1, here[0], here[1], here[2]], local_sem.at[0])
    own_prim = pltpu.make_async_copy(send.at[0], buf_ref.at[0, 0, 0, 0], local_sem.at[1])
    own_meta = pltpu.make_async_copy(meta_ref, all_meta_ref.at[here[0], here[1], here[2]], local_sem.at[2])
    own_extra.start()
    own_prim.start()
    own_meta.start()

    def held(p, stage, coords):
        done = ORDERS[p][:stage]
        spot = [pl.ds(0, SIDE) if a in done else coords[a] for a in range(3)]
        return spot

    def ext_copy(p, stage, delta, back):
        axis = ORDERS[p][stage]
        coords = list(here)
        if back:
            coords[axis] = (here[axis] - delta) % SIDE
        z, y, x = held(p, stage, coords)
        slab = buf_ref.at[1, z, y, x, :, pl.ds(p * part, part)]
        source = extra.at[:, pl.ds(p * part, part)] if stage == 0 else slab
        if back:
            source = slab
        to = list(here)
        to[axis] = (here[axis] + delta) % SIDE
        return pltpu.make_async_remote_copy(
            src_ref=source, dst_ref=slab,
            send_sem=ext_send.at[p, stage, delta - 1], recv_sem=ext_recv.at[p, stage, delta - 1],
            device_id=(lane_of(to), ctx), device_id_type=MESH)

    def meta_copy(stage, delta, back):
        axis = ORDERS[0][stage]
        coords = list(here)
        if back:
            coords[axis] = (here[axis] - delta) % SIDE
        z, y, x = held(0, stage, coords)
        slab = all_meta_ref.at[z, y, x]
        to = list(here)
        to[axis] = (here[axis] + delta) % SIDE
        source = meta_ref if stage == 0 and not back else slab
        return pltpu.make_async_remote_copy(
            src_ref=source, dst_ref=slab,
            send_sem=meta_send.at[stage, delta - 1], recv_sem=meta_recv.at[stage, delta - 1],
            device_id=(lane_of(to), ctx), device_id_type=MESH)

    def start_stage(stage):
        for delta in (1, 3, 2):
            meta_copy(stage, delta, False).start()
            for p in range(3):
                ext_copy(p, stage, delta, False).start()

    def end_stage(stage):
        for delta in (1, 3, 2):
            meta_copy(stage, delta, True).wait_recv()
            for p in range(3):
                ext_copy(p, stage, delta, True).wait_recv()

    def post(k, carry):
        offset = lax.rem(k * 21, LANES)
        d = coords_of(offset)
        pltpu.make_async_remote_copy(
            src_ref=send.at[offset], dst_ref=buf_ref.at[0, d[0], d[1], d[2]],
            send_sem=send_sem, recv_sem=recv_sem,
            device_id=(peer(offset), ctx), device_id_type=MESH).start()
        return carry

    start_stage(0)
    lax.fori_loop(1, 22, post, 0)
    own_extra.wait()
    own_meta.wait()
    end_stage(0)
    start_stage(1)
    lax.fori_loop(22, 43, post, 0)
    end_stage(1)
    start_stage(2)
    lax.fori_loop(43, LANES, post, 0)
    end_stage(2)
    own_prim.wait()
    for stage in range(3):
        for delta in (1, 3, 2):
            meta_copy(stage, delta, False).wait_send()
            for p in range(3):
                ext_copy(p, stage, delta, False).wait_send()


    first = pltpu.make_async_remote_copy(
        src_ref=send.at[pl.ds(1, LANES - 1)], dst_ref=send.at[pl.ds(1, LANES - 1)],
        send_sem=send_sem, recv_sem=recv_sem,
        device_id=(peer(1), ctx), device_id_type=MESH)
    first.wait_send()
    first.wait_recv()


def route(idx, meta, blocks):
    width = blocks.shape[2]
    return pl.pallas_call(
        route_kernel,
        out_shape=(
            jax.ShapeDtypeStruct((2, SIDE, SIDE, SIDE, BLK, width), jnp.bfloat16),
            jax.ShapeDtypeStruct((SIDE, SIDE, SIDE, 2, 128), jnp.int32),
        ),
        in_specs=[
            pl.BlockSpec(memory_space=pltpu.SMEM),
            pl.BlockSpec(memory_space=pltpu.VMEM),
            pl.BlockSpec(memory_space=pltpu.VMEM),
        ],
        out_specs=(pl.BlockSpec(memory_space=pl.ANY), pl.BlockSpec(memory_space=pl.ANY)),
        scratch_shapes=[
            pltpu.VMEM((LANES, BLK, width), jnp.bfloat16),
            pltpu.VMEM((BLK, width), jnp.bfloat16),
            pltpu.SemaphoreType.DMA,
            pltpu.SemaphoreType.DMA,
            pltpu.SemaphoreType.DMA((3, 3, 3)),
            pltpu.SemaphoreType.DMA((3, 3, 3)),
            pltpu.SemaphoreType.DMA((3, 3)),
            pltpu.SemaphoreType.DMA((3, 3)),
            pltpu.SemaphoreType.DMA((3,)),
        ],
        compiler_params=pltpu.CompilerParams(
            collective_id=0, has_side_effects=True, vmem_limit_bytes=16 << 20
        ),
        name="route",
    )(idx, meta, blocks)


def dot_nn(left, right):
    return jnp.dot(left, right, preferred_element_type=jnp.float32)


def dot_nt(left, right):
    return lax.dot_general(left, right, (((1,), (1,)), ((), ())), preferred_element_type=jnp.float32)


def dot_tn(left, right):
    return lax.dot_general(left, right, (((0,), (0,)), ((), ())), preferred_element_type=jnp.float32)


def row_scale(values):
    return lax.rsqrt(jnp.mean(values * values, axis=-1, keepdims=True) + 1e-06)


def order_row(meta, me):
    source = lax.broadcasted_iota(jnp.int32, (LANES, 128), 0)
    spot = lax.broadcasted_iota(jnp.int32, (LANES, 128), 1)
    usual = (meta[1] != me).astype(jnp.int32)
    double = (meta[0] == me).astype(jnp.int32)
    upto = usual + double
    shift = 1
    while shift < LANES:
        upto = upto + jnp.where(source >= shift, pltpu.roll(upto, shift, axis=0), 0)
        shift *= 2
    start = upto - usual - double
    slot = (
        ((me // 16 - source // 16) % SIDE) * 16
        + ((me // 4 - source // 4) % SIDE) * 4
        + (me - source) % SIDE
    )
    picks = jnp.where((usual == 1) & (start == spot), slot, 0)
    picks = picks + jnp.where((double == 1) & (start + usual == spot), source + LANES, 0)
    return jnp.sum(picks, axis=0, keepdims=True)


def scene_kernel(meta_ref, buf_ref, wq_ref, wk_ref, wv_ref, rate_ref, gate_ref, up_ref, down_ref, gain_ref, out_ref,
                 tokens, row_buf, table, queries, keys, values, term, hidden, grad, grad_down, gu_w, down_w,
                 other_gu, other_down, sums, other_sums,
                 sems, key_send, key_recv, val_send, val_recv, sum_send, sum_recv, w_send, w_recv):
    me = lax.axis_index("lane")
    ctx = lax.axis_index("ctx")
    mate = (me, 1 - ctx)
    width = tokens.shape[2]
    half = width // 2
    rows_all = LANES * BLK
    chunk = 256
    chunks = rows_all // chunk
    blocks = chunk // BLK
    step_size = 0.5 * width ** (-0.5)

    barrier = pltpu.get_barrier_semaphore()
    pl.semaphore_signal(barrier, inc=1, device_id=mate, device_id_type=MESH)

    row_buf[...] = order_row([meta_ref[:, 0, :], meta_ref[:, 1, :]], me)
    to_table = pltpu.make_async_copy(row_buf, table, sems)
    to_table.start()
    to_table.wait()

    def fetch(r, carry):
        tokens[r] = buf_ref[table[0, r]]
        return carry

    mine = pl.ds(pl.multiple_of(ctx * half, 128), half)
    gu_w[0, pl.ds(0, half), :] = gate_ref[:, mine].T
    gu_w[0, pl.ds(half, half), :] = up_ref[:, mine].T
    down_w[0] = down_ref[mine, :]

    def share(ref, send, recv, seg, c):
        part = ref.at[seg, pl.ds(c * chunk, chunk)]
        return pltpu.make_async_remote_copy(
            src_ref=part, dst_ref=part, send_sem=send.at[c], recv_sem=recv.at[c],
            device_id=mate, device_id_type=MESH)

    pl.semaphore_wait(barrier, 1)

    def load(c):
        x = tokens[pl.ds(c * blocks, blocks)].reshape(chunk, width)
        return x, pl.ds(c * chunk, chunk)

    def project(c, carry):
        lax.fori_loop(c * blocks, (c + 1) * blocks, fetch, 0)
        x, rows = load(c)
        k = dot_nn(x, wk_ref[...])
        keys[ctx, rows, :] = (k * row_scale(k)).astype(jnp.bfloat16)
        share(keys, key_send, key_recv, ctx, c).start()
        rate = dot_nn(x, rate_ref[...])
        rate = jnp.maximum(rate, 0.0) + jnp.log1p(jnp.exp(-jnp.abs(rate)))
        v = dot_nn(x, wv_ref[...])
        values[ctx, rows, :] = (rate[:, :1] * v).astype(jnp.bfloat16)
        share(values, val_send, val_recv, ctx, c).start()
        return carry

    lax.fori_loop(0, chunks, project, 0)

    def ask(c, carry):
        x, rows = load(c)
        q = dot_nn(x, wq_ref[...])
        queries[rows, :] = (q * row_scale(q)).astype(jnp.bfloat16)
        return carry

    lax.fori_loop(0, chunks, ask, 0)

    def arrived():
        def one(c, carry):
            share(keys, key_send, key_recv, 1 - ctx, c).wait_recv()
            share(values, val_send, val_recv, 1 - ctx, c).wait_recv()
            return carry

        lax.fori_loop(0, chunks, one, 0)

    def share_sums(seg):
        return pltpu.make_async_remote_copy(
            src_ref=sums.at[seg], dst_ref=other_sums.at[seg], send_sem=sum_send.at[seg], recv_sem=sum_recv.at[seg],
            device_id=mate, device_id_type=MESH)

    def share_weights(seg):
        return (
            pltpu.make_async_remote_copy(
                src_ref=gu_w.at[seg + 1], dst_ref=other_gu, send_sem=w_send.at[0], recv_sem=w_recv.at[0],
                device_id=mate, device_id_type=MESH),
            pltpu.make_async_remote_copy(
                src_ref=down_w.at[seg + 1], dst_ref=other_down, send_sem=w_send.at[1], recv_sem=w_recv.at[1],
                device_id=mate, device_id_type=MESH),
        )

    def update(seg):
        def terms(c, carry):
            rows = pl.ds(c * chunk, chunk)
            pre = dot_nt(keys[seg, rows, :], gu_w[seg])
            back = dot_nt(values[seg, rows, :], down_w[seg])
            gate_pre, up_pre = pre[:, :half], pre[:, half:]
            gate_sig = jax.nn.sigmoid(gate_pre)
            gated = gate_pre * gate_sig
            hidden[rows, :] = (gated * up_pre).astype(jnp.bfloat16)
            term[rows, pl.ds(0, half)] = (
                back * up_pre * gate_sig * (1.0 + gate_pre * (1.0 - gate_sig))
            ).astype(jnp.bfloat16)
            term[rows, pl.ds(half, half)] = (back * gated).astype(jnp.bfloat16)
            return carry

        lax.fori_loop(0, chunks, terms, 0)

        def slopes(j, carry):
            cols = pl.ds(pl.multiple_of(j * half, 128), half)
            g = dot_tn(term[:, cols], keys[seg])
            grad[pl.ds(j * half, half), :] = g
            sums[seg, pl.ds(j, 1), :] = jnp.sum(g * g, axis=0, keepdims=True)
            return carry

        lax.fori_loop(0, 2, slopes, 0)
        share_sums(seg).start()
        grad_down[...] = dot_tn(hidden[...], values[seg])
        g = grad_down[...]
        down_w[seg + 1] = (
            down_w[seg].astype(jnp.float32) + step_size * g * row_scale(g)
        ).astype(jnp.bfloat16)
        share_sums(seg).wait_recv()
        for j in range(2):
            rows = pl.ds(j * half, half)
            total = sums[seg, pl.ds(j, 1), :] + other_sums[seg, pl.ds(j, 1), :]
            scale = step_size * lax.rsqrt(total * (1.0 / width) + 1e-06)
            gu_w[seg + 1, rows, :] = (
                gu_w[seg, rows, :].astype(jnp.float32) + grad[rows, :] * scale
            ).astype(jnp.bfloat16)

    @pl.when(ctx == 1)
    def _():
        arrived()

    update(0)

    @pl.when(ctx == 1)
    def _():
        for copy in share_weights(0):
            copy.start()

    @pl.when(ctx == 0)
    def _():
        arrived()

    update(1)

    @pl.when(ctx == 0)
    def _():
        for copy in share_weights(1):
            copy.start()

    def answer_half(rows, gu):
        pre = dot_nt(queries[rows, :], gu)
        q_gate, q_up = pre[:, :half], pre[:, half:]
        return (q_gate * jax.nn.sigmoid(q_gate) * q_up).astype(jnp.bfloat16)

    def answer_own(c, carry):
        rows = pl.ds(c * chunk, chunk)
        hidden[rows, :] = answer_half(rows, gu_w[ctx + 1])
        return carry

    lax.fori_loop(0, chunks, answer_own, 0)
    for copy in share_weights(0):
        copy.wait_recv()

    def answer(c, carry):
        rows = pl.ds(c * chunk, chunk)
        y = dot_nn(hidden[rows, :], down_w[ctx + 1])
        y = y + dot_nn(answer_half(rows, other_gu[...]), other_down[...])
        out_ref[rows, :] = (y * row_scale(y) * gain_ref[...]).astype(jnp.bfloat16)
        return carry

    lax.fori_loop(0, chunks, answer, 0)

    def sent(c, carry):
        share(keys, key_send, key_recv, ctx, c).wait_send()
        share(values, val_send, val_recv, ctx, c).wait_send()
        return carry

    lax.fori_loop(0, chunks, sent, 0)
    for seg in range(2):
        share_sums(seg).wait_send()
    for copy in share_weights(0):
        copy.wait_send()


def scene(meta, buf, *operands):
    width = buf.shape[2]
    rows = LANES * BLK
    half = width // 2
    vmem = pl.BlockSpec(memory_space=pltpu.VMEM)
    bf, f32, dma = jnp.bfloat16, jnp.float32, pltpu.SemaphoreType.DMA
    return pl.pallas_call(
        scene_kernel,
        out_shape=jax.ShapeDtypeStruct((rows, width), bf),
        in_specs=[vmem] * (2 + len(operands)),
        out_specs=vmem,
        scratch_shapes=[
            pltpu.VMEM((LANES, BLK, width), bf),
            pltpu.VMEM((1, 128), jnp.int32),
            pltpu.SMEM((1, 128), jnp.int32),
            pltpu.VMEM((rows, width), bf),
            pltpu.VMEM((2, rows, width), bf),
            pltpu.VMEM((2, rows, width), bf),
            pltpu.VMEM((rows, width), bf),
            pltpu.VMEM((rows, half), bf),
            pltpu.VMEM((width, width), f32),
            pltpu.VMEM((half, width), f32),
            pltpu.VMEM((3, width, width), bf),
            pltpu.VMEM((3, half, width), bf),
            pltpu.VMEM((width, width), bf),
            pltpu.VMEM((half, width), bf),
            pltpu.VMEM((2, 8, width), f32),
            pltpu.VMEM((2, 8, width), f32),
            dma, dma((4,)), dma((4,)), dma((4,)), dma((4,)), dma((2,)), dma((2,)), dma((2,)), dma((2,)),
        ],
        compiler_params=pltpu.CompilerParams(
            collective_id=1, has_side_effects=True, vmem_limit_bytes=56 << 20
        ),
        name="scene",
    )(meta, buf, *operands)


def body(
    view_tokens,
    destinations,
    w_query,
    w_key,
    w_value,
    rate_vector,
    fast_gate,
    fast_up,
    fast_down,
    out_gain,
):
    width = view_tokens.shape[2]
    blocks = view_tokens[0].reshape(LANES, BLK, width)
    lane_ids = jnp.arange(LANES, dtype=jnp.int32)
    named = destinations[0][:, None] == lane_ids[None, :]
    first = jnp.min(jnp.where(named, lane_ids[:, None], LANES), axis=0)
    last = jnp.max(jnp.where(named, lane_ids[:, None], -1), axis=0)
    twice = last > first
    extra = jnp.max(jnp.where(twice, last, -1))
    doubled = jnp.max(jnp.where(twice, lane_ids, -1))
    missed = jnp.max(jnp.where(first == LANES, lane_ids, -1))
    columns = jnp.arange(128, dtype=jnp.int32)
    idx = jnp.where(columns < LANES, jnp.pad(jnp.minimum(first, LANES - 1), (0, 64)), extra)
    meta = jnp.broadcast_to(jnp.stack([doubled, missed])[:, None], (2, 128))
    buf, all_meta = route(idx, meta, blocks)
    rate = jnp.broadcast_to(rate_vector[:, None], (width, 128))
    out = scene(
        all_meta.reshape(LANES, 2, 128), buf.reshape(2 * LANES, BLK, width), w_query, w_key, w_value, rate,
        fast_gate, fast_up, fast_down, out_gain[None, :]
    )
    return out[None]


def solution(mesh):
    placed = (P("lane", "ctx", None), P("lane", "ctx"), P(), P(), P(), P(), P(), P(), P(), P())
    return jax.shard_map(
        body, mesh=mesh, in_specs=placed, out_specs=P("lane", "ctx", None), check_vma=False
    )
```

```python
import jax
import jax.numpy as jnp
from jax import lax
from jax.experimental import pallas as pl
from jax.experimental.pallas import tpu as pltpu
from jax.sharding import PartitionSpec as P

MESH = pl.DeviceIdType.MESH
LANES = 64
BLK = 16
SIDE = 4
GROUPS = 4
SPREAD = 21
GATHER = 61
ORDERS = ((2, 1, 0), (0, 2, 1), (1, 0, 2))


def coords_of(lane):
    return (lane // 16, (lane // 4) % 4, lane % 4)


def lane_of(coords):
    return coords[0] * 16 + coords[1] * 4 + coords[2]


def dot_nn(left, right):
    return jnp.dot(left, right, preferred_element_type=jnp.float32)


def dot_nt(left, right):
    return lax.dot_general(left, right, (((1,), (1,)), ((), ())), preferred_element_type=jnp.float32)


def dot_tn(left, right):
    return lax.dot_general(left, right, (((0,), (0,)), ((), ())), preferred_element_type=jnp.float32)


def row_scale(values):
    return lax.rsqrt(jnp.mean(values * values, axis=-1, keepdims=True) + 1e-06)


def spread(row):
    return jnp.broadcast_to(row, (128, 128)).T[:LANES]


def prefix(counts, source):
    upto = counts
    shift = 1
    while shift < LANES:
        upto = upto + jnp.where(source >= shift, pltpu.roll(upto, shift, axis=0), 0)
        shift *= 2
    return upto - counts


def send_rows(dest_row):
    block = lax.broadcasted_iota(jnp.int32, (LANES, 128), 0)
    lane = lax.broadcasted_iota(jnp.int32, (LANES, 128), 1)
    lane_row = lax.broadcasted_iota(jnp.int32, (1, 128), 1)
    named = spread(dest_row) == lane
    count = jnp.sum(named.astype(jnp.int32), axis=0, keepdims=True)
    total = jnp.sum(jnp.where(named, block, 0), axis=0, keepdims=True)
    first = jnp.min(jnp.where(named, block, LANES - 1), axis=0, keepdims=True)

    def of(mask, value):
        return jnp.sum(spread(jnp.where(mask, value, 0)), axis=0, keepdims=True)

    twice = count == 2
    absent = (count == 0) & (lane_row < LANES)
    return first, of(twice, total - first), of(twice, lane_row), of(absent, lane_row)


def order_rows(doubled, missed, me):
    source = lax.broadcasted_iota(jnp.int32, (LANES, 128), 0)
    spot = lax.broadcasted_iota(jnp.int32, (LANES, 128), 1)
    usual = (missed != me).astype(jnp.int32)
    hole = 1 - usual
    double = (doubled == me).astype(jnp.int32)
    start = prefix(usual + double, source)
    hole_rank = prefix(hole, source)
    double_rank = prefix(double, source)
    offset = (
        ((me // 16 - source // 16) % SIDE) * 16
        + ((me // 4 - source // 4) % SIDE) * 4
        + (me - source) % SIDE
    )
    slot = (offset * GATHER) % LANES

    def row(mask, value):
        return jnp.sum(jnp.where(mask, value, 0), axis=0, keepdims=True)

    by_source = row(source == spot, hole_rank)
    filler = (double == 1) & (double_rank == by_source)
    return (
        row(source == spot, usual),
        row(filler, source // 16),
        row(filler, (source // 4) % SIDE),
        row(filler, source % SIDE),
        row((hole == 1) & (hole_rank == spot), slot),
        row((usual == 1) & (start == spot), slot)
        + row((double == 1) & (start + usual == spot), double_rank + LANES),
    )


def scene_kernel(view_hbm, dest_hbm, wq_hbm, wk_hbm, wv_hbm, rate_hbm, gate_hbm, up_hbm, down_hbm, gain_hbm,
                 out_ref, order_ref,
                 view, dest, wq, wk, wv, rate_row, gate, up, down, gain, rate_w,
                 idx_v, idx_s, rows_v, rows_s, send, prim, ext, metas,
                 tokens, queries, keys, values, term, hidden, grad, grad_down, gu_w, down_w,
                 other_gu, other_down, sums, other_sums, result,
                 load_sem, local_sem, send_sem, recv_sem, ext_send, ext_recv, meta_send, meta_recv,
                 key_send, key_recv, val_send, val_recv, sum_send, sum_recv, w_send, w_recv):
    me = lax.axis_index("lane")
    ctx = lax.axis_index("ctx")
    here = coords_of(me)
    mate = (me, 1 - ctx)
    width = tokens.shape[1]
    half = width // 2
    part = width // 3
    chunk = tokens.shape[0] // GROUPS
    blocks = chunk // BLK
    step_size = 0.5 * width ** (-0.5)

    barrier = pltpu.get_barrier_semaphore()

    def greet(k, carry):
        pl.semaphore_signal(barrier, inc=1, device_id=(lax.rem(me + k, LANES), ctx), device_id_type=MESH)
        return carry

    lax.fori_loop(1, LANES, greet, 0)
    pl.semaphore_signal(barrier, inc=1, device_id=mate, device_id_type=MESH)

    loads = [
        pltpu.make_async_copy(a, b, load_sem.at[i])
        for i, (a, b) in enumerate((
            (dest_hbm, dest), (view_hbm, view), (wk_hbm, wk), (wv_hbm, wv), (wq_hbm, wq), (gate_hbm, gate),
            (up_hbm, up), (down_hbm, down), (rate_hbm, rate_row), (gain_hbm, gain)))
    ]
    for copy in loads:
        copy.start()
    loads[0].wait()

    first, second, doubled, missed = send_rows(jnp.concatenate([dest[...], dest[...]], axis=1))
    idx_v[0:1, :] = first
    idx_v[1:2, :] = second
    metas[here[0], here[1], here[2], 0:1, :] = doubled
    metas[here[0], here[1], here[2], 1:2, :] = missed
    to_idx = pltpu.make_async_copy(idx_v, idx_s, local_sem.at[0])
    to_idx.start()
    to_idx.wait()
    loads[1].wait()

    def block_of(b):
        return view[b]

    def peer(k):
        d = coords_of(lax.rem(k * SPREAD, LANES))
        return lane_of([(h + o) % SIDE for h, o in zip(here, d)])

    ext[here[0], here[1], here[2]] = block_of(idx_s[1, 0])
    prim[0] = block_of(idx_s[0, me])

    def pack(k, carry):
        send[k] = block_of(idx_s[0, peer(k)])
        return carry

    lax.fori_loop(1, LANES, pack, 0)
    pl.semaphore_wait(barrier, LANES)

    def stage_copy(ref, tail, order, stage, delta, back, sends, recvs):
        axis = order[stage]
        spot = list(here)
        if back:
            spot[axis] = (here[axis] - delta) % SIDE
        for done in order[:stage]:
            spot[done] = pl.ds(0, SIDE)
        to = list(here)
        to[axis] = (here[axis] + delta) % SIDE
        slab = ref.at[(*spot, *tail)]
        return pltpu.make_async_remote_copy(
            src_ref=slab, dst_ref=slab, send_sem=sends, recv_sem=recvs,
            device_id=(lane_of(to), ctx), device_id_type=MESH)

    def stage_copies(stage, back):
        made = []
        for delta in (1, 3, 2):
            made.append(stage_copy(
                metas, (), ORDERS[0], stage, delta, back,
                meta_send.at[stage, delta - 1], meta_recv.at[stage, delta - 1]))
            for p in range(3):
                made.append(stage_copy(
                    ext, (slice(None), pl.ds(p * part, part)), ORDERS[p], stage, delta, back,
                    ext_send.at[p, stage, delta - 1], ext_recv.at[p, stage, delta - 1]))
        return made

    def start_stage(stage):
        for copy in stage_copies(stage, False):
            copy.start()

    def end_stage(stage):
        for copy in stage_copies(stage, True):
            copy.wait_recv()

    def post(k, carry):
        pltpu.make_async_remote_copy(
            src_ref=send.at[k], dst_ref=prim.at[k],
            send_sem=send_sem, recv_sem=recv_sem.at[k // blocks],
            device_id=(peer(k), ctx), device_id_type=MESH).start()
        return carry

    start_stage(0)
    lax.fori_loop(1, 8, post, 0)
    for copy in loads[2:]:
        copy.wait()
    mine = pl.ds(pl.multiple_of(ctx * half, 128), half)
    gu_w[0, pl.ds(0, half), :] = gate[:, mine].T
    gu_w[0, pl.ds(half, half), :] = up[:, mine].T
    down_w[0] = down[mine, :]
    rate_w[...] = jnp.broadcast_to(rate_row[...].astype(jnp.float32), (128, width)).T.astype(jnp.bfloat16)
    end_stage(0)
    start_stage(1)
    lax.fori_loop(8, 16, post, 0)
    end_stage(1)
    start_stage(2)
    lax.fori_loop(16, LANES, post, 0)
    end_stage(2)

    table = metas[...].reshape(LANES, 2, 128)
    for i, row in enumerate(order_rows(table[:, 0, :], table[:, 1, :], me)):
        rows_v[i:i + 1, :] = row
    to_rows = pltpu.make_async_copy(rows_v, rows_s, local_sem.at[0])
    to_rows.start()
    to_order = pltpu.make_async_copy(rows_v, order_ref, local_sem.at[1])
    to_order.start()
    to_rows.wait()

    def share(ref, sends, recvs, seg, c):
        piece = ref.at[seg, pl.ds(c * chunk, chunk)]
        return pltpu.make_async_remote_copy(
            src_ref=piece, dst_ref=piece, send_sem=sends.at[c], recv_sem=recvs.at[c],
            device_id=mate, device_id_type=MESH)

    def fill(k, carry):
        d = coords_of(lax.rem(k * SPREAD, LANES))
        s = lane_of([(h - o) % SIDE for h, o in zip(here, d)])
        keep = rows_s[0, s].astype(jnp.float32)
        doubled_block = ext[rows_s[1, s], rows_s[2, s], rows_s[3, s]].astype(jnp.float32)
        block = prim[k].astype(jnp.float32) * keep + doubled_block * (1.0 - keep)
        tokens[pl.ds(pl.multiple_of(k * BLK, BLK), BLK), :] = block.astype(jnp.bfloat16)
        return carry

    def landed(lo, count, g):
        piece = prim.at[pl.ds(lo, count)]
        pltpu.make_async_remote_copy(
            src_ref=piece, dst_ref=piece, send_sem=send_sem, recv_sem=recv_sem.at[g],
            device_id=mate, device_id_type=MESH).wait_recv()

    def from_mate(c):
        share(keys, key_send, key_recv, 1 - ctx, c).wait_recv()
        share(values, val_send, val_recv, 1 - ctx, c).wait_recv()

    def terms(seg, c):
        rows = pl.ds(c * chunk, chunk)
        pre = dot_nt(keys[seg, rows, :], gu_w[seg])
        back = dot_nt(values[seg, rows, :], down_w[seg])
        gate_pre, up_pre = pre[:, :half], pre[:, half:]
        gate_sig = jax.nn.sigmoid(gate_pre)
        gated = gate_pre * gate_sig
        hidden[rows, :] = (gated * up_pre).astype(jnp.bfloat16)
        term[rows, pl.ds(0, half)] = (
            back * up_pre * gate_sig * (1.0 + gate_pre * (1.0 - gate_sig))
        ).astype(jnp.bfloat16)
        term[rows, pl.ds(half, half)] = (back * gated).astype(jnp.bfloat16)

    def first_terms(c):
        @pl.when(ctx == 1)
        def _():
            from_mate(c)

        terms(0, c)

    def project(c, carry):
        @pl.when(c == 0)
        def _():
            landed(1, blocks - 1, 0)

        @pl.when(c > 0)
        def _():
            landed(c * blocks, blocks, c)

        lax.fori_loop(c * blocks, (c + 1) * blocks, fill, 0)
        rows = pl.ds(c * chunk, chunk)
        x = tokens[rows, :]
        k = dot_nn(x, wk[...])
        keys[ctx, rows, :] = (k * row_scale(k)).astype(jnp.bfloat16)
        share(keys, key_send, key_recv, ctx, c).start()
        rate = dot_nn(x, rate_w[...])
        rate = jnp.maximum(rate, 0.0) + jnp.log1p(jnp.exp(-jnp.abs(rate)))
        v = dot_nn(x, wv[...])
        values[ctx, rows, :] = (rate[:, :1] * v).astype(jnp.bfloat16)
        share(values, val_send, val_recv, ctx, c).start()
        q = dot_nn(x, wq[...])
        queries[rows, :] = (q * row_scale(q)).astype(jnp.bfloat16)

        @pl.when(c > 0)
        def _():
            first_terms(c - 1)

        return carry

    lax.fori_loop(0, GROUPS, project, 0)
    first_terms(GROUPS - 1)

    def share_sums(seg):
        return pltpu.make_async_remote_copy(
            src_ref=sums.at[seg], dst_ref=other_sums.at[seg], send_sem=sum_send.at[seg], recv_sem=sum_recv.at[seg],
            device_id=mate, device_id_type=MESH)

    def share_weights(seg):
        return (
            pltpu.make_async_remote_copy(
                src_ref=gu_w.at[seg + 1], dst_ref=other_gu, send_sem=w_send.at[0], recv_sem=w_recv.at[0],
                device_id=mate, device_id_type=MESH),
            pltpu.make_async_remote_copy(
                src_ref=down_w.at[seg + 1], dst_ref=other_down, send_sem=w_send.at[1], recv_sem=w_recv.at[1],
                device_id=mate, device_id_type=MESH),
        )

    def renew(seg):
        def slopes(j, carry):
            cols = pl.ds(pl.multiple_of(j * half, 128), half)
            g = dot_tn(term[:, cols], keys[seg])
            grad[pl.ds(j * half, half), :] = g
            sums[seg, pl.ds(j, 1), :] = jnp.sum(g * g, axis=0, keepdims=True)
            return carry

        lax.fori_loop(0, 2, slopes, 0)
        share_sums(seg).start()
        grad_down[...] = dot_tn(hidden[...], values[seg])
        g = grad_down[...]
        down_w[seg + 1] = (
            down_w[seg].astype(jnp.float32) + step_size * g * row_scale(g)
        ).astype(jnp.bfloat16)
        share_sums(seg).wait_recv()
        for j in range(2):
            rows = pl.ds(j * half, half)
            total = sums[seg, pl.ds(j, 1), :] + other_sums[seg, pl.ds(j, 1), :]
            scale = step_size * lax.rsqrt(total * (1.0 / width) + 1e-06)
            gu_w[seg + 1, rows, :] = (
                gu_w[seg, rows, :].astype(jnp.float32) + grad[rows, :] * scale
            ).astype(jnp.bfloat16)

    renew(0)

    @pl.when(ctx == 1)
    def _():
        for copy in share_weights(0):
            copy.start()

    @pl.when(ctx == 0)
    def _():
        def one(c, carry):
            from_mate(c)
            return carry

        lax.fori_loop(0, GROUPS, one, 0)

    def second_terms(c, carry):
        terms(1, c)
        return carry

    lax.fori_loop(0, GROUPS, second_terms, 0)
    renew(1)

    @pl.when(ctx == 0)
    def _():
        for copy in share_weights(1):
            copy.start()

    def answer_half(rows, gu):
        pre = dot_nt(queries[rows, :], gu)
        q_gate, q_up = pre[:, :half], pre[:, half:]
        return (q_gate * jax.nn.sigmoid(q_gate) * q_up).astype(jnp.bfloat16)

    def answer_own(c, carry):
        rows = pl.ds(c * chunk, chunk)
        hidden[rows, :] = answer_half(rows, gu_w[ctx + 1])
        return carry

    lax.fori_loop(0, GROUPS, answer_own, 0)
    for copy in share_weights(0):
        copy.wait_recv()

    def out_copy(c):
        rows = pl.ds(c * chunk, chunk)
        return pltpu.make_async_copy(result.at[rows], out_ref.at[rows], load_sem.at[c])

    def answer(c, carry):
        rows = pl.ds(c * chunk, chunk)
        y = dot_nn(hidden[rows, :], down_w[ctx + 1])
        y = y + dot_nn(answer_half(rows, other_gu[...]), other_down[...])
        result[rows, :] = (y * row_scale(y) * gain[...]).astype(jnp.bfloat16)
        out_copy(c).start()
        return carry

    lax.fori_loop(0, GROUPS, answer, 0)

    def sent(c, carry):
        share(keys, key_send, key_recv, ctx, c).wait_send()
        share(values, val_send, val_recv, ctx, c).wait_send()
        out_copy(c).wait()
        return carry

    lax.fori_loop(0, GROUPS, sent, 0)
    for seg in range(2):
        share_sums(seg).wait_send()
    for copy in share_weights(0):
        copy.wait_send()
    for stage in range(3):
        for copy in stage_copies(stage, False):
            copy.wait_send()
    to_order.wait()
    piece = send.at[pl.ds(1, LANES - 1)]
    pltpu.make_async_remote_copy(
        src_ref=piece, dst_ref=piece, send_sem=send_sem, recv_sem=recv_sem.at[0],
        device_id=mate, device_id_type=MESH).wait_send()


def scene(*operands):
    width = operands[0].shape[2]
    rows = LANES * BLK
    half = width // 2
    any_ = pl.BlockSpec(memory_space=pl.ANY)
    bf, f32, i32, dma, vmem = jnp.bfloat16, jnp.float32, jnp.int32, pltpu.SemaphoreType.DMA, pltpu.VMEM
    square = vmem((width, width), bf)
    return pl.pallas_call(
        scene_kernel,
        out_shape=(jax.ShapeDtypeStruct((rows, width), bf), jax.ShapeDtypeStruct((8, 128), i32)),
        in_specs=[any_] * len(operands),
        out_specs=(any_, any_),
        scratch_shapes=[
            vmem((LANES, BLK, width), bf), vmem((1, LANES), i32), square, square, square, vmem((1, width), bf),
            square, square, square, vmem((1, width), f32), vmem((width, 128), bf),
            vmem((8, 128), i32), pltpu.SMEM((8, 128), i32), vmem((8, 128), i32), pltpu.SMEM((8, 128), i32),
            vmem((LANES, BLK, width), bf), vmem((LANES, BLK, width), bf),
            vmem((SIDE, SIDE, SIDE, BLK, width), bf), vmem((SIDE, SIDE, SIDE, 2, 128), i32),
            vmem((rows, width), bf), vmem((rows, width), bf),
            vmem((2, rows, width), bf), vmem((2, rows, width), bf), vmem((rows, width), bf), vmem((rows, half), bf),
            vmem((width, width), f32), vmem((half, width), f32),
            vmem((3, width, width), bf), vmem((3, half, width), bf),
            square, vmem((half, width), bf), vmem((2, 8, width), f32), vmem((2, 8, width), f32), vmem((rows, width), bf),
            dma((10,)), dma((2,)), dma, dma((GROUPS,)),
            dma((3, 3, 3)), dma((3, 3, 3)), dma((3, 3)), dma((3, 3)),
            dma((4,)), dma((4,)), dma((4,)), dma((4,)), dma((2,)), dma((2,)), dma((2,)), dma((2,)),
        ],
        compiler_params=pltpu.CompilerParams(
            collective_id=0, has_side_effects=True, vmem_limit_bytes=60 << 20
        ),
        name="scene",
    )(*operands)


def settle_kernel(order_ref, blocks_ref, out_ref, sem):
    def move(r, carry):
        code = order_ref[5, r]
        slot = jnp.where(code < LANES, code, order_ref[4, jnp.maximum(code - LANES, 0)])
        pltpu.make_async_copy(blocks_ref.at[slot], out_ref.at[r], sem).start()
        return carry

    lax.fori_loop(0, LANES, move, 0)
    pltpu.make_async_copy(blocks_ref, out_ref, sem).wait()


def settle(order, blocks):
    return pl.pallas_call(
        settle_kernel,
        out_shape=jax.ShapeDtypeStruct(blocks.shape, blocks.dtype),
        in_specs=[pl.BlockSpec(memory_space=pltpu.SMEM), pl.BlockSpec(memory_space=pl.ANY)],
        out_specs=pl.BlockSpec(memory_space=pl.ANY),
        scratch_shapes=[pltpu.SemaphoreType.DMA],
        name="settle",
    )(order, blocks)


def body(view_tokens, destinations, w_query, w_key, w_value, rate_vector, fast_gate, fast_up, fast_down, out_gain):
    width = view_tokens.shape[2]
    slots, order = scene(
        view_tokens.reshape(LANES, BLK, width), destinations, w_query, w_key, w_value, rate_vector[None, :],
        fast_gate, fast_up, fast_down, out_gain[None, :]
    )
    out = settle(order, slots.reshape(LANES, BLK, width))
    return out.reshape(1, LANES * BLK, width)


def solution(mesh):
    placed = (P("lane", "ctx", None), P("lane", "ctx"), P(), P(), P(), P(), P(), P(), P(), P())
    return jax.shard_map(
        body, mesh=mesh, in_specs=placed, out_specs=P("lane", "ctx", None), check_vma=False
    )
```

```python
import jax
import jax.numpy as jnp
from jax import lax
from jax.experimental import pallas as pl
from jax.experimental.pallas import tpu as pltpu
from jax.sharding import PartitionSpec as P

MESH = pl.DeviceIdType.MESH
LANES = 64
BLK = 16
SIDE = 4
GROUPS = 4
SPREAD = 21
GATHER = 61
ORDERS = ((2, 1, 0), (0, 2, 1), (1, 0, 2))


def coords_of(lane):
    return (lane // 16, (lane // 4) % 4, lane % 4)


def lane_of(coords):
    return coords[0] * 16 + coords[1] * 4 + coords[2]


def dot_nn(left, right):
    return jnp.dot(left, right, preferred_element_type=jnp.float32)


def dot_nt(left, right):
    return lax.dot_general(left, right, (((1,), (1,)), ((), ())), preferred_element_type=jnp.float32)


def dot_tn(left, right):
    return lax.dot_general(left, right, (((0,), (0,)), ((), ())), preferred_element_type=jnp.float32)


def row_scale(values):
    return lax.rsqrt(jnp.mean(values * values, axis=-1, keepdims=True) + 1e-06)


def spread(row):
    return jnp.broadcast_to(row, (128, 128)).T[:LANES]


def prefix(counts, source):
    upto = counts
    shift = 1
    while shift < LANES:
        upto = upto + jnp.where(source >= shift, pltpu.roll(upto, shift, axis=0), 0)
        shift *= 2
    return upto - counts


def send_rows(dest_row):
    block = lax.broadcasted_iota(jnp.int32, (LANES, 128), 0)
    lane = lax.broadcasted_iota(jnp.int32, (LANES, 128), 1)
    lane_row = lax.broadcasted_iota(jnp.int32, (1, 128), 1)
    named = spread(dest_row) == lane
    count = jnp.sum(named.astype(jnp.int32), axis=0, keepdims=True)
    total = jnp.sum(jnp.where(named, block, 0), axis=0, keepdims=True)
    first = jnp.min(jnp.where(named, block, LANES - 1), axis=0, keepdims=True)

    def of(mask, value):
        return jnp.sum(spread(jnp.where(mask, value, 0)), axis=0, keepdims=True)

    twice = count == 2
    absent = (count == 0) & (lane_row < LANES)
    return first, of(twice, total - first), of(twice, lane_row), of(absent, lane_row)


def order_rows(doubled, missed, me):
    source = lax.broadcasted_iota(jnp.int32, (LANES, 128), 0)
    spot = lax.broadcasted_iota(jnp.int32, (LANES, 128), 1)
    usual = (missed != me).astype(jnp.int32)
    hole = 1 - usual
    double = (doubled == me).astype(jnp.int32)
    start = prefix(usual + double, source)
    hole_rank = prefix(hole, source)
    double_rank = prefix(double, source)
    offset = (
        ((me // 16 - source // 16) % SIDE) * 16
        + ((me // 4 - source // 4) % SIDE) * 4
        + (me - source) % SIDE
    )
    slot = (offset * GATHER) % LANES

    def row(mask, value):
        return jnp.sum(jnp.where(mask, value, 0), axis=0, keepdims=True)

    by_source = row(source == spot, hole_rank)
    filler = (double == 1) & (double_rank == by_source)
    return (
        row(source == spot, usual),
        row(filler, source // 16),
        row(filler, (source // 4) % SIDE),
        row(filler, source % SIDE),
        row((hole == 1) & (hole_rank == spot), slot),
        row((usual == 1) & (start == spot), slot)
        + row((double == 1) & (start + usual == spot), double_rank + LANES),
    )


def scene_kernel(view_hbm, dest_hbm, wq_hbm, wk_hbm, wv_hbm, rate_hbm, gate_hbm, up_hbm, down_hbm, gain_hbm,
                 out_ref, order_ref,
                 view, dest, wq, wk, wv, rate_row, gate, up, down, gain, rate_w,
                 idx_v, idx_s, rows_v, rows_s, send, prim, ext, metas,
                 tokens, queries, keys, values, term, hidden, grad, grad_down, gu_w, down_w,
                 other_gu, other_down, sums, other_sums, result,
                 load_sem, local_sem, send_sem, recv_sem, ext_send, ext_recv, meta_send, meta_recv,
                 key_send, key_recv, val_send, val_recv, sum_send, sum_recv, w_send, w_recv):
    me = lax.axis_index("lane")
    ctx = lax.axis_index("ctx")
    here = coords_of(me)
    mate = (me, 1 - ctx)
    width = tokens.shape[1]
    half = width // 2
    part = width // 3
    chunk = tokens.shape[0] // GROUPS
    blocks = chunk // BLK
    step_size = 0.5 * width ** (-0.5)

    barrier = pltpu.get_barrier_semaphore()

    def greet(k, carry):
        pl.semaphore_signal(barrier, inc=1, device_id=(lax.rem(me + k, LANES), ctx), device_id_type=MESH)
        return carry

    lax.fori_loop(1, LANES, greet, 0)
    pl.semaphore_signal(barrier, inc=1, device_id=mate, device_id_type=MESH)

    loads = [
        pltpu.make_async_copy(a, b, load_sem.at[i])
        for i, (a, b) in enumerate((
            (dest_hbm, dest), (view_hbm, view), (wk_hbm, wk), (wv_hbm, wv), (wq_hbm, wq), (gate_hbm, gate),
            (up_hbm, up), (down_hbm, down), (rate_hbm, rate_row), (gain_hbm, gain)))
    ]
    for copy in loads:
        copy.start()
    loads[0].wait()

    first, second, doubled, missed = send_rows(jnp.concatenate([dest[...], dest[...]], axis=1))
    idx_v[0:1, :] = first
    idx_v[1:2, :] = second
    metas[here[0], here[1], here[2], 0:1, :] = doubled
    metas[here[0], here[1], here[2], 1:2, :] = missed
    to_idx = pltpu.make_async_copy(idx_v, idx_s, local_sem.at[0])
    to_idx.start()
    to_idx.wait()
    loads[1].wait()

    def block_of(b):
        return view[b]

    def peer(k):
        d = coords_of(lax.rem(k * SPREAD, LANES))
        return lane_of([(h + o) % SIDE for h, o in zip(here, d)])

    ext[here[0], here[1], here[2]] = block_of(idx_s[1, 0])
    prim[0] = block_of(idx_s[0, me])

    def pack(k, carry):
        send[k] = block_of(idx_s[0, peer(k)])
        return carry

    lax.fori_loop(1, LANES, pack, 0)
    pl.semaphore_wait(barrier, LANES)

    def stage_copy(ref, tail, order, stage, delta, back, sends, recvs):
        axis = order[stage]
        spot = list(here)
        if back:
            spot[axis] = (here[axis] - delta) % SIDE
        for done in order[:stage]:
            spot[done] = pl.ds(0, SIDE)
        to = list(here)
        to[axis] = (here[axis] + delta) % SIDE
        slab = ref.at[(*spot, *tail)]
        return pltpu.make_async_remote_copy(
            src_ref=slab, dst_ref=slab, send_sem=sends, recv_sem=recvs,
            device_id=(lane_of(to), ctx), device_id_type=MESH)

    def stage_copies(stage, back):
        made = []
        for delta in (1, 3, 2):
            made.append(stage_copy(
                metas, (), ORDERS[0], stage, delta, back,
                meta_send.at[stage, delta - 1], meta_recv.at[stage, delta - 1]))
            for p in range(3):
                made.append(stage_copy(
                    ext, (slice(None), pl.ds(p * part, part)), ORDERS[p], stage, delta, back,
                    ext_send.at[p, stage, delta - 1], ext_recv.at[p, stage, delta - 1]))
        return made

    def start_stage(stage):
        for copy in stage_copies(stage, False):
            copy.start()

    def end_stage(stage):
        for copy in stage_copies(stage, True):
            copy.wait_recv()

    def post(k, carry):
        pltpu.make_async_remote_copy(
            src_ref=send.at[k], dst_ref=prim.at[k],
            send_sem=send_sem, recv_sem=recv_sem.at[k // blocks],
            device_id=(peer(k), ctx), device_id_type=MESH).start()
        return carry

    start_stage(0)
    lax.fori_loop(1, 8, post, 0)
    for copy in loads[2:]:
        copy.wait()
    mine = pl.ds(pl.multiple_of(ctx * half, 128), half)
    gu_w[0, pl.ds(0, half), :] = gate[:, mine].T
    gu_w[0, pl.ds(half, half), :] = up[:, mine].T
    down_w[0] = down[mine, :]
    rate_w[...] = jnp.broadcast_to(rate_row[...].astype(jnp.float32), (128, width)).T.astype(jnp.bfloat16)
    end_stage(0)
    start_stage(1)
    lax.fori_loop(8, 16, post, 0)
    end_stage(1)
    start_stage(2)
    lax.fori_loop(16, LANES, post, 0)
    end_stage(2)

    table = metas[...].reshape(LANES, 2, 128)
    for i, row in enumerate(order_rows(table[:, 0, :], table[:, 1, :], me)):
        rows_v[i:i + 1, :] = row
    to_rows = pltpu.make_async_copy(rows_v, rows_s, local_sem.at[0])
    to_rows.start()
    to_order = pltpu.make_async_copy(rows_v, order_ref, local_sem.at[1])
    to_order.start()
    to_rows.wait()

    def share(ref, sends, recvs, seg, c):
        piece = ref.at[seg, pl.ds(c * chunk, chunk)]
        return pltpu.make_async_remote_copy(
            src_ref=piece, dst_ref=piece, send_sem=sends.at[c], recv_sem=recvs.at[c],
            device_id=mate, device_id_type=MESH)

    def fill(k, carry):
        d = coords_of(lax.rem(k * SPREAD, LANES))
        s = lane_of([(h - o) % SIDE for h, o in zip(here, d)])
        keep = rows_s[0, s].astype(jnp.float32)
        doubled_block = ext[rows_s[1, s], rows_s[2, s], rows_s[3, s]].astype(jnp.float32)
        block = prim[k].astype(jnp.float32) * keep + doubled_block * (1.0 - keep)
        tokens[pl.ds(pl.multiple_of(k * BLK, BLK), BLK), :] = block.astype(jnp.bfloat16)
        return carry

    def landed(lo, count, g):
        piece = prim.at[pl.ds(lo, count)]
        pltpu.make_async_remote_copy(
            src_ref=piece, dst_ref=piece, send_sem=send_sem, recv_sem=recv_sem.at[g],
            device_id=mate, device_id_type=MESH).wait_recv()

    def from_mate(c):
        share(keys, key_send, key_recv, 1 - ctx, c).wait_recv()
        share(values, val_send, val_recv, 1 - ctx, c).wait_recv()

    def terms(seg, c):
        rows = pl.ds(c * chunk, chunk)
        pre = dot_nt(keys[seg, rows, :], gu_w[seg])
        back = dot_nt(values[seg, rows, :], down_w[seg])
        gate_pre, up_pre = pre[:, :half], pre[:, half:]
        gate_sig = jax.nn.sigmoid(gate_pre)
        gated = gate_pre * gate_sig
        hidden[rows, :] = (gated * up_pre).astype(jnp.bfloat16)
        term[rows, pl.ds(0, half)] = (
            back * up_pre * gate_sig * (1.0 + gate_pre * (1.0 - gate_sig))
        ).astype(jnp.bfloat16)
        term[rows, pl.ds(half, half)] = (back * gated).astype(jnp.bfloat16)

    def first_terms(c):
        @pl.when(ctx == 1)
        def _():
            from_mate(c)

        terms(0, c)

    def project(c, carry):
        @pl.when(c == 0)
        def _():
            landed(1, blocks - 1, 0)

        @pl.when(c > 0)
        def _():
            landed(c * blocks, blocks, c)

        lax.fori_loop(c * blocks, (c + 1) * blocks, fill, 0)
        rows = pl.ds(c * chunk, chunk)
        x = tokens[rows, :]
        k = dot_nn(x, wk[...])
        keys[ctx, rows, :] = (k * row_scale(k)).astype(jnp.bfloat16)
        share(keys, key_send, key_recv, ctx, c).start()
        rate = dot_nn(x, rate_w[...])
        rate = jnp.maximum(rate, 0.0) + jnp.log1p(jnp.exp(-jnp.abs(rate)))
        v = dot_nn(x, wv[...])
        values[ctx, rows, :] = (rate[:, :1] * v).astype(jnp.bfloat16)
        share(values, val_send, val_recv, ctx, c).start()
        q = dot_nn(x, wq[...])
        queries[rows, :] = (q * row_scale(q)).astype(jnp.bfloat16)

        @pl.when(c > 0)
        def _():
            first_terms(c - 1)

        return carry

    lax.fori_loop(0, GROUPS, project, 0)
    first_terms(GROUPS - 1)

    def share_sums(seg):
        return pltpu.make_async_remote_copy(
            src_ref=sums.at[seg], dst_ref=other_sums.at[seg], send_sem=sum_send.at[seg], recv_sem=sum_recv.at[seg],
            device_id=mate, device_id_type=MESH)

    def share_weights(seg):
        return (
            pltpu.make_async_remote_copy(
                src_ref=gu_w.at[seg + 1], dst_ref=other_gu, send_sem=w_send.at[0], recv_sem=w_recv.at[0],
                device_id=mate, device_id_type=MESH),
            pltpu.make_async_remote_copy(
                src_ref=down_w.at[seg + 1], dst_ref=other_down, send_sem=w_send.at[1], recv_sem=w_recv.at[1],
                device_id=mate, device_id_type=MESH),
        )

    def renew(seg):
        def slopes(j, carry):
            cols = pl.ds(pl.multiple_of(j * half, 128), half)
            g = dot_tn(term[:, cols], keys[seg])
            grad[pl.ds(j * half, half), :] = g
            sums[seg, pl.ds(j, 1), :] = jnp.sum(g * g, axis=0, keepdims=True)
            return carry

        lax.fori_loop(0, 2, slopes, 0)
        share_sums(seg).start()
        grad_down[...] = dot_tn(hidden[...], values[seg])
        g = grad_down[...]
        down_w[seg + 1] = (
            down_w[seg].astype(jnp.float32) + step_size * g * row_scale(g)
        ).astype(jnp.bfloat16)
        share_sums(seg).wait_recv()
        for j in range(2):
            rows = pl.ds(j * half, half)
            total = sums[seg, pl.ds(j, 1), :] + other_sums[seg, pl.ds(j, 1), :]
            scale = step_size * lax.rsqrt(total * (1.0 / width) + 1e-06)
            gu_w[seg + 1, rows, :] = (
                gu_w[seg, rows, :].astype(jnp.float32) + grad[rows, :] * scale
            ).astype(jnp.bfloat16)

    renew(0)

    @pl.when(ctx == 1)
    def _():
        for copy in share_weights(0):
            copy.start()

    @pl.when(ctx == 0)
    def _():
        def one(c, carry):
            from_mate(c)
            return carry

        lax.fori_loop(0, GROUPS, one, 0)

    def second_terms(c, carry):
        terms(1, c)
        return carry

    lax.fori_loop(0, GROUPS, second_terms, 0)
    renew(1)

    @pl.when(ctx == 0)
    def _():
        for copy in share_weights(1):
            copy.start()

    def answer_half(rows, gu):
        pre = dot_nt(queries[rows, :], gu)
        q_gate, q_up = pre[:, :half], pre[:, half:]
        return (q_gate * jax.nn.sigmoid(q_gate) * q_up).astype(jnp.bfloat16)

    def answer_own(c, carry):
        rows = pl.ds(c * chunk, chunk)
        hidden[rows, :] = answer_half(rows, gu_w[ctx + 1])
        return carry

    lax.fori_loop(0, GROUPS, answer_own, 0)
    for copy in share_weights(0):
        copy.wait_recv()

    def out_copy(c):
        rows = pl.ds(c * chunk, chunk)
        return pltpu.make_async_copy(result.at[rows], out_ref.at[rows], load_sem.at[c])

    def answer(c, carry):
        rows = pl.ds(c * chunk, chunk)
        y = dot_nn(hidden[rows, :], down_w[ctx + 1])
        y = y + dot_nn(answer_half(rows, other_gu[...]), other_down[...])
        result[rows, :] = (y * row_scale(y) * gain[...]).astype(jnp.bfloat16)
        out_copy(c).start()
        return carry

    lax.fori_loop(0, GROUPS, answer, 0)

    def sent(c, carry):
        share(keys, key_send, key_recv, ctx, c).wait_send()
        share(values, val_send, val_recv, ctx, c).wait_send()
        out_copy(c).wait()
        return carry

    lax.fori_loop(0, GROUPS, sent, 0)
    for seg in range(2):
        share_sums(seg).wait_send()
    for copy in share_weights(0):
        copy.wait_send()
    for stage in range(3):
        for copy in stage_copies(stage, False):
            copy.wait_send()
    to_order.wait()
    piece = send.at[pl.ds(1, LANES - 1)]
    pltpu.make_async_remote_copy(
        src_ref=piece, dst_ref=piece, send_sem=send_sem, recv_sem=recv_sem.at[0],
        device_id=mate, device_id_type=MESH).wait_send()


def scene(*operands):
    width = operands[0].shape[2]
    rows = LANES * BLK
    half = width // 2
    any_ = pl.BlockSpec(memory_space=pl.ANY)
    bf, f32, i32, dma, vmem = jnp.bfloat16, jnp.float32, jnp.int32, pltpu.SemaphoreType.DMA, pltpu.VMEM
    square = vmem((width, width), bf)
    return pl.pallas_call(
        scene_kernel,
        out_shape=(jax.ShapeDtypeStruct((rows, width), bf), jax.ShapeDtypeStruct((8, 128), i32)),
        in_specs=[any_] * len(operands),
        out_specs=(any_, any_),
        scratch_shapes=[
            vmem((LANES, BLK, width), bf), vmem((1, LANES), i32), square, square, square, vmem((1, width), bf),
            square, square, square, vmem((1, width), f32), vmem((width, 128), bf),
            vmem((8, 128), i32), pltpu.SMEM((8, 128), i32), vmem((8, 128), i32), pltpu.SMEM((8, 128), i32),
            vmem((LANES, BLK, width), bf), vmem((LANES, BLK, width), bf),
            vmem((SIDE, SIDE, SIDE, BLK, width), bf), vmem((SIDE, SIDE, SIDE, 2, 128), i32),
            vmem((rows, width), bf), vmem((rows, width), bf),
            vmem((2, rows, width), bf), vmem((2, rows, width), bf), vmem((rows, width), bf), vmem((rows, half), bf),
            vmem((width, width), f32), vmem((half, width), f32),
            vmem((3, width, width), bf), vmem((3, half, width), bf),
            square, vmem((half, width), bf), vmem((2, 8, width), f32), vmem((2, 8, width), f32), vmem((rows, width), bf),
            dma((10,)), dma((2,)), dma, dma((GROUPS,)),
            dma((3, 3, 3)), dma((3, 3, 3)), dma((3, 3)), dma((3, 3)),
            dma((4,)), dma((4,)), dma((4,)), dma((4,)), dma((2,)), dma((2,)), dma((2,)), dma((2,)),
        ],
        compiler_params=pltpu.CompilerParams(
            collective_id=0, has_side_effects=True, vmem_limit_bytes=60 << 20
        ),
        name="scene",
    )(*operands)


def settle_kernel(order_ref, blocks_ref, out_ref, sem):
    def move(r, carry):
        code = order_ref[5, r]
        slot = jnp.where(code < LANES, code, order_ref[4, jnp.maximum(code - LANES, 0)])
        pltpu.make_async_copy(blocks_ref.at[slot], out_ref.at[r], sem).start()
        return carry

    lax.fori_loop(0, LANES, move, 0)
    pltpu.make_async_copy(blocks_ref, out_ref, sem).wait()


def settle(order, blocks):
    return pl.pallas_call(
        settle_kernel,
        out_shape=jax.ShapeDtypeStruct(blocks.shape, blocks.dtype),
        in_specs=[pl.BlockSpec(memory_space=pltpu.SMEM), pl.BlockSpec(memory_space=pltpu.VMEM)],
        out_specs=pl.BlockSpec(memory_space=pl.ANY),
        scratch_shapes=[pltpu.SemaphoreType.DMA],
        name="settle",
    )(order, blocks)


def body(view_tokens, destinations, w_query, w_key, w_value, rate_vector, fast_gate, fast_up, fast_down, out_gain):
    width = view_tokens.shape[2]
    slots, order = scene(
        view_tokens.reshape(LANES, BLK, width), destinations, w_query, w_key, w_value, rate_vector[None, :],
        fast_gate, fast_up, fast_down, out_gain[None, :]
    )
    out = settle(order, slots.reshape(LANES, BLK, width))
    return out.reshape(1, LANES * BLK, width)


def solution(mesh):
    placed = (P("lane", "ctx", None), P("lane", "ctx"), P(), P(), P(), P(), P(), P(), P(), P())
    return jax.shard_map(
        body, mesh=mesh, in_specs=placed, out_specs=P("lane", "ctx", None), check_vma=False
    )
```

```python
import jax
import jax.numpy as jnp
from jax import lax
from jax.experimental import pallas as pl
from jax.experimental.pallas import tpu as pltpu
from jax.sharding import PartitionSpec as P

MESH = pl.DeviceIdType.MESH
LANES = 64
BLK = 16
SIDE = 4
GROUPS = 4
SPREAD = 21
GATHER = 61
ORDERS = ((2, 1, 0), (0, 2, 1), (1, 0, 2))


def coords_of(lane):
    return (lane // 16, (lane // 4) % 4, lane % 4)


def lane_of(coords):
    return coords[0] * 16 + coords[1] * 4 + coords[2]


def dot_nn(left, right):
    return jnp.dot(left, right, preferred_element_type=jnp.float32)


def dot_nt(left, right):
    return lax.dot_general(left, right, (((1,), (1,)), ((), ())), preferred_element_type=jnp.float32)


def dot_tn(left, right):
    return lax.dot_general(left, right, (((0,), (0,)), ((), ())), preferred_element_type=jnp.float32)


def row_scale(values):
    return lax.rsqrt(jnp.mean(values * values, axis=-1, keepdims=True) + 1e-06)


def spread(row):
    return jnp.broadcast_to(row, (128, 128)).T[:LANES]


def prefix(counts, source):
    upto = counts
    shift = 1
    while shift < LANES:
        upto = upto + jnp.where(source >= shift, pltpu.roll(upto, shift, axis=0), 0)
        shift *= 2
    return upto - counts


def send_rows(dest_row):
    block = lax.broadcasted_iota(jnp.int32, (LANES, 128), 0)
    lane = lax.broadcasted_iota(jnp.int32, (LANES, 128), 1)
    lane_row = lax.broadcasted_iota(jnp.int32, (1, 128), 1)
    named = spread(dest_row) == lane
    count = jnp.sum(named.astype(jnp.int32), axis=0, keepdims=True)
    total = jnp.sum(jnp.where(named, block, 0), axis=0, keepdims=True)
    first = jnp.min(jnp.where(named, block, LANES - 1), axis=0, keepdims=True)

    def of(mask, value):
        return jnp.sum(spread(jnp.where(mask, value, 0)), axis=0, keepdims=True)

    twice = count == 2
    absent = (count == 0) & (lane_row < LANES)
    return first, of(twice, total - first), of(twice, lane_row), of(absent, lane_row)


def order_rows(doubled, missed, me):
    source = lax.broadcasted_iota(jnp.int32, (LANES, 128), 0)
    spot = lax.broadcasted_iota(jnp.int32, (LANES, 128), 1)
    usual = (missed != me).astype(jnp.int32)
    hole = 1 - usual
    double = (doubled == me).astype(jnp.int32)
    start = prefix(usual + double, source)
    hole_rank = prefix(hole, source)
    double_rank = prefix(double, source)
    offset = (
        ((me // 16 - source // 16) % SIDE) * 16
        + ((me // 4 - source // 4) % SIDE) * 4
        + (me - source) % SIDE
    )
    slot = (offset * GATHER) % LANES

    def row(mask, value):
        return jnp.sum(jnp.where(mask, value, 0), axis=0, keepdims=True)

    by_source = row(source == spot, hole_rank)
    filler = (double == 1) & (double_rank == by_source)
    return (
        row(source == spot, usual),
        row(filler, source // 16),
        row(filler, (source // 4) % SIDE),
        row(filler, source % SIDE),
        row((hole == 1) & (hole_rank == spot), slot),
        row((usual == 1) & (start == spot), slot)
        + row((double == 1) & (start + usual == spot), double_rank + LANES),
    )


def scene_kernel(view_hbm, dest_hbm, wq_hbm, wk_hbm, wv_hbm, rate_hbm, gate_hbm, up_hbm, down_hbm, gain_hbm,
                 out_ref, order_ref,
                 view, dest, wq, wk, wv, rate_row, gate, up, down, gain, rate_w,
                 idx_v, idx_s, rows_v, rows_s, send, prim, ext, metas,
                 tokens, queries, keys, values, term, hidden, grad, grad_down, gu_w, down_w,
                 other_gu, other_down, sums, other_sums, result,
                 load_sem, local_sem, send_sem, recv_sem, ext_send, ext_recv, meta_send, meta_recv,
                 key_send, key_recv, val_send, val_recv, sum_send, sum_recv, w_send, w_recv):
    me = lax.axis_index("lane")
    ctx = lax.axis_index("ctx")
    here = coords_of(me)
    mate = (me, 1 - ctx)
    width = tokens.shape[1]
    half = width // 2
    part = width // 3
    chunk = tokens.shape[0] // GROUPS
    blocks = chunk // BLK
    step_size = 0.5 * width ** (-0.5)

    barrier = pltpu.get_barrier_semaphore()

    def greet(k, carry):
        pl.semaphore_signal(barrier, inc=1, device_id=(lax.rem(me + k, LANES), ctx), device_id_type=MESH)
        return carry

    lax.fori_loop(1, LANES, greet, 0)
    pl.semaphore_signal(barrier, inc=1, device_id=mate, device_id_type=MESH)

    loads = [
        pltpu.make_async_copy(a, b, load_sem.at[i])
        for i, (a, b) in enumerate((
            (dest_hbm, dest), (view_hbm, view), (wk_hbm, wk), (wv_hbm, wv), (wq_hbm, wq), (gate_hbm, gate),
            (up_hbm, up), (down_hbm, down), (rate_hbm, rate_row), (gain_hbm, gain)))
    ]
    for copy in loads:
        copy.start()
    loads[0].wait()

    first, second, doubled, missed = send_rows(jnp.concatenate([dest[...], dest[...]], axis=1))
    idx_v[0:1, :] = first
    idx_v[1:2, :] = second
    metas[here[0], here[1], here[2], 0:1, :] = doubled
    metas[here[0], here[1], here[2], 1:2, :] = missed
    to_idx = pltpu.make_async_copy(idx_v, idx_s, local_sem.at[0])
    to_idx.start()
    to_idx.wait()
    loads[1].wait()

    def block_of(b):
        return view[b]

    def peer(k):
        d = coords_of(lax.rem(k * SPREAD, LANES))
        return lane_of([(h + o) % SIDE for h, o in zip(here, d)])

    ext[here[0], here[1], here[2]] = block_of(idx_s[1, 0])
    prim[0] = block_of(idx_s[0, me])

    def pack(k, carry):
        send[k] = block_of(idx_s[0, peer(k)])
        return carry

    lax.fori_loop(1, LANES, pack, 0)
    pl.semaphore_wait(barrier, LANES)

    def stage_copy(ref, tail, order, stage, delta, back, sends, recvs):
        axis = order[stage]
        spot = list(here)
        if back:
            spot[axis] = (here[axis] - delta) % SIDE
        for done in order[:stage]:
            spot[done] = pl.ds(0, SIDE)
        to = list(here)
        to[axis] = (here[axis] + delta) % SIDE
        slab = ref.at[(*spot, *tail)]
        return pltpu.make_async_remote_copy(
            src_ref=slab, dst_ref=slab, send_sem=sends, recv_sem=recvs,
            device_id=(lane_of(to), ctx), device_id_type=MESH)

    def stage_copies(stage, back):
        made = []
        for delta in (1, 3, 2):
            made.append(stage_copy(
                metas, (), ORDERS[0], stage, delta, back,
                meta_send.at[stage, delta - 1], meta_recv.at[stage, delta - 1]))
            for p in range(3):
                made.append(stage_copy(
                    ext, (slice(None), pl.ds(p * part, part)), ORDERS[p], stage, delta, back,
                    ext_send.at[p, stage, delta - 1], ext_recv.at[p, stage, delta - 1]))
        return made

    def start_stage(stage):
        for copy in stage_copies(stage, False):
            copy.start()

    def end_stage(stage):
        for copy in stage_copies(stage, True):
            copy.wait_recv()

    def post(k, carry):
        pltpu.make_async_remote_copy(
            src_ref=send.at[k], dst_ref=prim.at[k],
            send_sem=send_sem, recv_sem=recv_sem.at[k // blocks],
            device_id=(peer(k), ctx), device_id_type=MESH).start()
        return carry

    start_stage(0)
    lax.fori_loop(1, 8, post, 0)
    end_stage(0)
    start_stage(1)
    lax.fori_loop(8, 16, post, 0)
    end_stage(1)
    start_stage(2)
    lax.fori_loop(16, LANES, post, 0)
    for copy in loads[2:]:
        copy.wait()
    mine = pl.ds(pl.multiple_of(ctx * half, 128), half)
    gu_w[0, pl.ds(0, half), :] = gate[:, mine].T
    gu_w[0, pl.ds(half, half), :] = up[:, mine].T
    down_w[0] = down[mine, :]
    rate_w[...] = jnp.broadcast_to(rate_row[...].astype(jnp.float32).reshape(1, width), (128, width)).T.astype(jnp.bfloat16)
    end_stage(2)

    table = metas[...].reshape(LANES, 2, 128)
    for i, row in enumerate(order_rows(table[:, 0, :], table[:, 1, :], me)):
        rows_v[i:i + 1, :] = row
    to_rows = pltpu.make_async_copy(rows_v, rows_s, local_sem.at[0])
    to_rows.start()
    to_order = pltpu.make_async_copy(rows_v, order_ref, local_sem.at[1])
    to_order.start()
    to_rows.wait()

    def share(ref, sends, recvs, seg, c):
        piece = ref.at[seg, pl.ds(c * chunk, chunk)]
        return pltpu.make_async_remote_copy(
            src_ref=piece, dst_ref=piece, send_sem=sends.at[c], recv_sem=recvs.at[c],
            device_id=mate, device_id_type=MESH)

    def fill(k, carry):
        d = coords_of(lax.rem(k * SPREAD, LANES))
        s = lane_of([(h - o) % SIDE for h, o in zip(here, d)])
        keep = rows_s[0, s].astype(jnp.float32)
        doubled_block = ext[rows_s[1, s], rows_s[2, s], rows_s[3, s]].astype(jnp.float32)
        block = prim[k].astype(jnp.float32) * keep + doubled_block * (1.0 - keep)
        tokens[pl.ds(pl.multiple_of(k * BLK, BLK), BLK), :] = block.astype(jnp.bfloat16)
        return carry

    def landed(lo, count, g):
        piece = prim.at[pl.ds(lo, count)]
        pltpu.make_async_remote_copy(
            src_ref=piece, dst_ref=piece, send_sem=send_sem, recv_sem=recv_sem.at[g],
            device_id=mate, device_id_type=MESH).wait_recv()

    def from_mate(c):
        share(keys, key_send, key_recv, 1 - ctx, c).wait_recv()
        share(values, val_send, val_recv, 1 - ctx, c).wait_recv()

    def terms(seg, c):
        rows = pl.ds(c * chunk, chunk)
        pre = dot_nt(keys[seg, rows, :], gu_w[seg])
        back = dot_nt(values[seg, rows, :], down_w[seg])
        gate_pre, up_pre = pre[:, :half], pre[:, half:]
        gate_sig = jax.nn.sigmoid(gate_pre)
        gated = gate_pre * gate_sig
        hidden[rows, :] = (gated * up_pre).astype(jnp.bfloat16)
        term[rows, pl.ds(0, half)] = (
            back * up_pre * gate_sig * (1.0 + gate_pre * (1.0 - gate_sig))
        ).astype(jnp.bfloat16)
        term[rows, pl.ds(half, half)] = (back * gated).astype(jnp.bfloat16)

    def first_terms(c):
        @pl.when(ctx == 1)
        def _():
            from_mate(c)

        terms(0, c)

    def project(c, carry):
        @pl.when(c == 0)
        def _():
            landed(1, blocks - 1, 0)

        @pl.when(c > 0)
        def _():
            landed(c * blocks, blocks, c)

        lax.fori_loop(c * blocks, (c + 1) * blocks, fill, 0)
        rows = pl.ds(c * chunk, chunk)
        x = tokens[rows, :]
        k = dot_nn(x, wk[...])
        keys[ctx, rows, :] = (k * row_scale(k)).astype(jnp.bfloat16)
        share(keys, key_send, key_recv, ctx, c).start()
        rate = dot_nn(x, rate_w[...])
        rate = jnp.maximum(rate, 0.0) + jnp.log1p(jnp.exp(-jnp.abs(rate)))
        v = dot_nn(x, wv[...])
        values[ctx, rows, :] = (rate[:, :1] * v).astype(jnp.bfloat16)
        share(values, val_send, val_recv, ctx, c).start()
        q = dot_nn(x, wq[...])
        queries[rows, :] = (q * row_scale(q)).astype(jnp.bfloat16)

        @pl.when(c > 0)
        def _():
            first_terms(c - 1)

        return carry

    lax.fori_loop(0, GROUPS, project, 0)
    first_terms(GROUPS - 1)

    def share_sums(seg):
        return pltpu.make_async_remote_copy(
            src_ref=sums.at[seg], dst_ref=other_sums.at[seg], send_sem=sum_send.at[seg], recv_sem=sum_recv.at[seg],
            device_id=mate, device_id_type=MESH)

    def share_weights(seg):
        return (
            pltpu.make_async_remote_copy(
                src_ref=gu_w.at[seg + 1], dst_ref=other_gu, send_sem=w_send.at[0], recv_sem=w_recv.at[0],
                device_id=mate, device_id_type=MESH),
            pltpu.make_async_remote_copy(
                src_ref=down_w.at[seg + 1], dst_ref=other_down, send_sem=w_send.at[1], recv_sem=w_recv.at[1],
                device_id=mate, device_id_type=MESH),
        )

    def renew(seg):
        def slopes(j, carry):
            cols = pl.ds(pl.multiple_of(j * half, 128), half)
            g = dot_tn(term[:, cols], keys[seg])
            grad[pl.ds(j * half, half), :] = g
            sums[seg, pl.ds(j, 1), :] = jnp.sum(g * g, axis=0, keepdims=True)
            return carry

        lax.fori_loop(0, 2, slopes, 0)
        share_sums(seg).start()
        grad_down[...] = dot_tn(hidden[...], values[seg])
        g = grad_down[...]
        down_w[seg + 1] = (
            down_w[seg].astype(jnp.float32) + step_size * g * row_scale(g)
        ).astype(jnp.bfloat16)
        share_sums(seg).wait_recv()
        for j in range(2):
            rows = pl.ds(j * half, half)
            total = sums[seg, pl.ds(j, 1), :] + other_sums[seg, pl.ds(j, 1), :]
            scale = step_size * lax.rsqrt(total * (1.0 / width) + 1e-06)
            gu_w[seg + 1, rows, :] = (
                gu_w[seg, rows, :].astype(jnp.float32) + grad[rows, :] * scale
            ).astype(jnp.bfloat16)

    renew(0)

    @pl.when(ctx == 1)
    def _():
        for copy in share_weights(0):
            copy.start()

    @pl.when(ctx == 0)
    def _():
        def one(c, carry):
            from_mate(c)
            return carry

        lax.fori_loop(0, GROUPS, one, 0)

    def second_terms(c, carry):
        terms(1, c)
        return carry

    lax.fori_loop(0, GROUPS, second_terms, 0)
    renew(1)

    @pl.when(ctx == 0)
    def _():
        for copy in share_weights(1):
            copy.start()

    def answer_half(rows, gu):
        pre = dot_nt(queries[rows, :], gu)
        q_gate, q_up = pre[:, :half], pre[:, half:]
        return (q_gate * jax.nn.sigmoid(q_gate) * q_up).astype(jnp.bfloat16)

    def answer_own(c, carry):
        rows = pl.ds(c * chunk, chunk)
        hidden[rows, :] = answer_half(rows, gu_w[ctx + 1])
        return carry

    lax.fori_loop(0, GROUPS, answer_own, 0)
    for copy in share_weights(0):
        copy.wait_recv()

    def out_copy(c):
        rows = pl.ds(c * chunk, chunk)
        return pltpu.make_async_copy(result.at[rows], out_ref.at[rows], load_sem.at[c])

    def answer(c, carry):
        rows = pl.ds(c * chunk, chunk)
        y = dot_nn(hidden[rows, :], down_w[ctx + 1])
        y = y + dot_nn(answer_half(rows, other_gu[...]), other_down[...])
        result[rows, :] = (y * row_scale(y) * gain[...].reshape(1, width)).astype(jnp.bfloat16)
        out_copy(c).start()
        return carry

    lax.fori_loop(0, GROUPS, answer, 0)

    def sent(c, carry):
        share(keys, key_send, key_recv, ctx, c).wait_send()
        share(values, val_send, val_recv, ctx, c).wait_send()
        out_copy(c).wait()
        return carry

    lax.fori_loop(0, GROUPS, sent, 0)
    for seg in range(2):
        share_sums(seg).wait_send()
    for copy in share_weights(0):
        copy.wait_send()
    for stage in range(3):
        for copy in stage_copies(stage, False):
            copy.wait_send()
    to_order.wait()
    piece = send.at[pl.ds(1, LANES - 1)]
    pltpu.make_async_remote_copy(
        src_ref=piece, dst_ref=piece, send_sem=send_sem, recv_sem=recv_sem.at[0],
        device_id=mate, device_id_type=MESH).wait_send()


def scene(*operands):
    width = operands[0].shape[2]
    rows = LANES * BLK
    half = width // 2
    any_ = pl.BlockSpec(memory_space=pl.ANY)
    bf, f32, i32, dma, vmem = jnp.bfloat16, jnp.float32, jnp.int32, pltpu.SemaphoreType.DMA, pltpu.VMEM
    square = vmem((width, width), bf)
    return pl.pallas_call(
        scene_kernel,
        out_shape=(jax.ShapeDtypeStruct((rows, width), bf), jax.ShapeDtypeStruct((8, 128), i32)),
        in_specs=[any_] * len(operands),
        out_specs=(any_, any_),
        scratch_shapes=[
            vmem((LANES, BLK, width), bf), vmem((1, LANES), i32), square, square, square, vmem((width,), bf),
            square, square, square, vmem((width,), f32), vmem((width, 128), bf),
            vmem((8, 128), i32), pltpu.SMEM((8, 128), i32), vmem((8, 128), i32), pltpu.SMEM((8, 128), i32),
            vmem((LANES, BLK, width), bf), vmem((LANES, BLK, width), bf),
            vmem((SIDE, SIDE, SIDE, BLK, width), bf), vmem((SIDE, SIDE, SIDE, 2, 128), i32),
            vmem((rows, width), bf), vmem((rows, width), bf),
            vmem((2, rows, width), bf), vmem((2, rows, width), bf), vmem((rows, width), bf), vmem((rows, half), bf),
            vmem((width, width), f32), vmem((half, width), f32),
            vmem((3, width, width), bf), vmem((3, half, width), bf),
            square, vmem((half, width), bf), vmem((2, 8, width), f32), vmem((2, 8, width), f32), vmem((rows, width), bf),
            dma((10,)), dma((2,)), dma, dma((GROUPS,)),
            dma((3, 3, 3)), dma((3, 3, 3)), dma((3, 3)), dma((3, 3)),
            dma((4,)), dma((4,)), dma((4,)), dma((4,)), dma((2,)), dma((2,)), dma((2,)), dma((2,)),
        ],
        compiler_params=pltpu.CompilerParams(
            collective_id=0, has_side_effects=True, vmem_limit_bytes=60 << 20
        ),
        name="scene",
    )(*operands)


def settle_kernel(order_ref, blocks_ref, out_ref, sem):
    def move(r, carry):
        code = order_ref[5, r]
        slot = jnp.where(code < LANES, code, order_ref[4, jnp.maximum(code - LANES, 0)])
        pltpu.make_async_copy(blocks_ref.at[slot], out_ref.at[r], sem).start()
        return carry

    lax.fori_loop(0, LANES, move, 0)
    pltpu.make_async_copy(blocks_ref, out_ref, sem).wait()


def settle(order, blocks):
    return pl.pallas_call(
        settle_kernel,
        out_shape=jax.ShapeDtypeStruct(blocks.shape, blocks.dtype),
        in_specs=[pl.BlockSpec(memory_space=pltpu.SMEM), pl.BlockSpec(memory_space=pltpu.VMEM)],
        out_specs=pl.BlockSpec(memory_space=pl.ANY),
        scratch_shapes=[pltpu.SemaphoreType.DMA],
        name="settle",
    )(order, blocks)


def body(view_tokens, destinations, w_query, w_key, w_value, rate_vector, fast_gate, fast_up, fast_down, out_gain):
    width = view_tokens.shape[2]
    slots, order = scene(
        view_tokens.reshape(LANES, BLK, width), destinations, w_query, w_key, w_value, rate_vector,
        fast_gate, fast_up, fast_down, out_gain
    )
    out = settle(order, slots.reshape(LANES, BLK, width))
    return out.reshape(1, LANES * BLK, width)


def solution(mesh):
    placed = (P("lane", "ctx", None), P("lane", "ctx"), P(), P(), P(), P(), P(), P(), P(), P())
    return jax.shard_map(
        body, mesh=mesh, in_specs=placed, out_specs=P("lane", "ctx", None), check_vma=False
    )
```

```python
import jax
import jax.numpy as jnp
from jax import lax
from jax.experimental import pallas as pl
from jax.experimental.pallas import tpu as pltpu
from jax.sharding import PartitionSpec as P

MESH = pl.DeviceIdType.MESH
LANES = 64
BLK = 16
SIDE = 4
GROUPS = 4
ORDERS = ((2, 1, 0), (0, 2, 1), (1, 0, 2))


def coords_of(lane):
    return (lane // 16, (lane // 4) % 4, lane % 4)


def lane_of(coords):
    return coords[0] * 16 + coords[1] * 4 + coords[2]


def dot_nn(left, right):
    return jnp.dot(left, right, preferred_element_type=jnp.float32)


def dot_nt(left, right):
    return lax.dot_general(left, right, (((1,), (1,)), ((), ())), preferred_element_type=jnp.float32)


def dot_tn(left, right):
    return lax.dot_general(left, right, (((0,), (0,)), ((), ())), preferred_element_type=jnp.float32)


def row_scale(values):
    return lax.rsqrt(jnp.mean(values * values, axis=-1, keepdims=True) + 1e-06)


def offset_of(k):
    dz, dy = (k // 4) % SIDE, k % SIDE
    return dz, dy, (k // 16 + 2 * SIDE - dz - dy) % SIDE


def spread(row):
    return jnp.broadcast_to(row, (128, 128)).T[:LANES]


def prefix(counts, source):
    upto = counts
    shift = 1
    while shift < LANES:
        upto = upto + jnp.where(source >= shift, pltpu.roll(upto, shift, axis=0), 0)
        shift *= 2
    return upto - counts


def send_rows(dest_row):
    block = lax.broadcasted_iota(jnp.int32, (LANES, 128), 0)
    lane = lax.broadcasted_iota(jnp.int32, (LANES, 128), 1)
    lane_row = lax.broadcasted_iota(jnp.int32, (1, 128), 1)
    named = spread(dest_row) == lane
    count = jnp.sum(named.astype(jnp.int32), axis=0, keepdims=True)
    total = jnp.sum(jnp.where(named, block, 0), axis=0, keepdims=True)
    first = jnp.min(jnp.where(named, block, LANES - 1), axis=0, keepdims=True)

    def of(mask, value):
        return jnp.sum(spread(jnp.where(mask, value, 0)), axis=0, keepdims=True)

    twice = count == 2
    absent = (count == 0) & (lane_row < LANES)
    return first, of(twice, total - first), of(twice, lane_row), of(absent, lane_row)


def order_rows(doubled, missed, me):
    source = lax.broadcasted_iota(jnp.int32, (LANES, 128), 0)
    spot = lax.broadcasted_iota(jnp.int32, (LANES, 128), 1)
    usual = (missed != me).astype(jnp.int32)
    hole = 1 - usual
    double = (doubled == me).astype(jnp.int32)
    start = prefix(usual + double, source)
    hole_rank = prefix(hole, source)
    double_rank = prefix(double, source)
    dz, dy, dx = (me // 16 - source // 16) % SIDE, (me // 4 - source // 4) % SIDE, (me - source) % SIDE
    slot = ((dz + dy + dx) % SIDE) * 16 + dz * 4 + dy

    def row(mask, value):
        return jnp.sum(jnp.where(mask, value, 0), axis=0, keepdims=True)

    by_source = row(source == spot, hole_rank)
    filler = (double == 1) & (double_rank == by_source)
    return (
        row(source == spot, usual),
        row(filler, source // 16),
        row(filler, (source // 4) % SIDE),
        row(filler, source % SIDE),
        row((hole == 1) & (hole_rank == spot), slot),
        row((usual == 1) & (start == spot), slot)
        + row((double == 1) & (start + usual == spot), double_rank + LANES),
    )


def scene_kernel(view_hbm, dest_hbm, wq_hbm, wk_hbm, wv_hbm, rate_hbm, gate_hbm, up_hbm, down_hbm, gain_hbm,
                 out_ref, order_ref,
                 view, dest, wq, wk, wv, rate_row, gate, up, down, gain, rate_w,
                 idx_v, idx_s, rows_v, rows_s, send, prim, ext, metas,
                 tokens, queries, keys, values, term, hidden, grad, grad_down, gu_w, down_w,
                 other_gu, other_down, sums, other_sums, result,
                 load_sem, local_sem, send_sem, recv_sem, ext_send, ext_recv, meta_send, meta_recv,
                 key_send, key_recv, val_send, val_recv, sum_send, sum_recv, w_send, w_recv):
    me = lax.axis_index("lane")
    ctx = lax.axis_index("ctx")
    here = coords_of(me)
    mate = (me, 1 - ctx)
    width = tokens.shape[1]
    half = width // 2
    part = width // 3
    chunk = tokens.shape[0] // GROUPS
    blocks = chunk // BLK
    step_size = 0.5 * width ** (-0.5)

    barrier = pltpu.get_barrier_semaphore()

    def greet(k, carry):
        pl.semaphore_signal(barrier, inc=1, device_id=(lax.rem(me + k, LANES), ctx), device_id_type=MESH)
        return carry

    lax.fori_loop(1, LANES, greet, 0)
    pl.semaphore_signal(barrier, inc=1, device_id=mate, device_id_type=MESH)

    loads = [
        pltpu.make_async_copy(a, b, load_sem.at[i])
        for i, (a, b) in enumerate((
            (dest_hbm, dest), (view_hbm, view), (wk_hbm, wk), (wv_hbm, wv), (wq_hbm, wq), (gate_hbm, gate),
            (up_hbm, up), (down_hbm, down), (rate_hbm, rate_row), (gain_hbm, gain)))
    ]
    for copy in loads:
        copy.start()
    loads[0].wait()

    first, second, doubled, missed = send_rows(jnp.concatenate([dest[...], dest[...]], axis=1))
    idx_v[0:1, :] = first
    idx_v[1:2, :] = second
    metas[here[0], here[1], here[2], 0:1, :] = doubled
    metas[here[0], here[1], here[2], 1:2, :] = missed
    to_idx = pltpu.make_async_copy(idx_v, idx_s, local_sem.at[0])
    to_idx.start()
    to_idx.wait()
    loads[1].wait()

    def block_of(b):
        return view[b]

    def peer(k):
        d = offset_of(k)
        return lane_of([(h + o) % SIDE for h, o in zip(here, d)])

    ext[here[0], here[1], here[2]] = block_of(idx_s[1, 0])
    prim[0] = block_of(idx_s[0, me])

    def pack(k, carry):
        send[k] = block_of(idx_s[0, peer(k)])
        return carry

    lax.fori_loop(1, LANES, pack, 0)
    pl.semaphore_wait(barrier, LANES)

    def stage_copy(ref, tail, order, stage, delta, back, sends, recvs):
        axis = order[stage]
        spot = list(here)
        if back:
            spot[axis] = (here[axis] - delta) % SIDE
        for done in order[:stage]:
            spot[done] = pl.ds(0, SIDE)
        to = list(here)
        to[axis] = (here[axis] + delta) % SIDE
        slab = ref.at[(*spot, *tail)]
        return pltpu.make_async_remote_copy(
            src_ref=slab, dst_ref=slab, send_sem=sends, recv_sem=recvs,
            device_id=(lane_of(to), ctx), device_id_type=MESH)

    def stage_copies(stage, back):
        made = []
        for delta in (1, 3, 2):
            made.append(stage_copy(
                metas, (), ORDERS[0], stage, delta, back,
                meta_send.at[stage, delta - 1], meta_recv.at[stage, delta - 1]))
            for p in range(3):
                made.append(stage_copy(
                    ext, (slice(None), pl.ds(p * part, part)), ORDERS[p], stage, delta, back,
                    ext_send.at[p, stage, delta - 1], ext_recv.at[p, stage, delta - 1]))
        return made

    def start_stage(stage):
        for copy in stage_copies(stage, False):
            copy.start()

    def end_stage(stage):
        for copy in stage_copies(stage, True):
            copy.wait_recv()

    def post(k, carry):
        pltpu.make_async_remote_copy(
            src_ref=send.at[k], dst_ref=prim.at[k],
            send_sem=send_sem, recv_sem=recv_sem.at[k // blocks],
            device_id=(peer(k), ctx), device_id_type=MESH).start()
        return carry

    start_stage(0)
    lax.fori_loop(1, blocks, post, 0)
    end_stage(0)
    start_stage(1)
    end_stage(1)
    start_stage(2)
    for copy in loads[2:]:
        copy.wait()
    mine = pl.ds(pl.multiple_of(ctx * half, 128), half)
    gu_w[0, pl.ds(0, half), :] = gate[:, mine].T
    gu_w[0, pl.ds(half, half), :] = up[:, mine].T
    down_w[0] = down[mine, :]
    rate_w[...] = jnp.broadcast_to(rate_row[...].astype(jnp.float32).reshape(1, width), (128, width)).T.astype(jnp.bfloat16)
    end_stage(2)
    lax.fori_loop(blocks, LANES, post, 0)
    table = metas[...].reshape(LANES, 2, 128)
    for i, row in enumerate(order_rows(table[:, 0, :], table[:, 1, :], me)):
        rows_v[i:i + 1, :] = row
    to_rows = pltpu.make_async_copy(rows_v, rows_s, local_sem.at[0])
    to_rows.start()
    to_order = pltpu.make_async_copy(rows_v, order_ref, local_sem.at[1])
    to_order.start()
    to_rows.wait()

    def share(ref, sends, recvs, seg, c):
        piece = ref.at[seg, pl.ds(c * chunk, chunk)]
        return pltpu.make_async_remote_copy(
            src_ref=piece, dst_ref=piece, send_sem=sends.at[c], recv_sem=recvs.at[c],
            device_id=mate, device_id_type=MESH)

    def fill(k, carry):
        d = offset_of(k)
        s = lane_of([(h - o) % SIDE for h, o in zip(here, d)])
        keep = rows_s[0, s].astype(jnp.float32)
        doubled_block = ext[rows_s[1, s], rows_s[2, s], rows_s[3, s]].astype(jnp.float32)
        block = prim[k].astype(jnp.float32) * keep + doubled_block * (1.0 - keep)
        tokens[pl.ds(pl.multiple_of(k * BLK, BLK), BLK), :] = block.astype(jnp.bfloat16)
        return carry

    def landed(lo, count, g):
        piece = prim.at[pl.ds(lo, count)]
        pltpu.make_async_remote_copy(
            src_ref=piece, dst_ref=piece, send_sem=send_sem, recv_sem=recv_sem.at[g],
            device_id=mate, device_id_type=MESH).wait_recv()

    def from_mate(c):
        share(keys, key_send, key_recv, 1 - ctx, c).wait_recv()
        share(values, val_send, val_recv, 1 - ctx, c).wait_recv()

    def terms(seg, c):
        rows = pl.ds(c * chunk, chunk)
        pre = dot_nt(keys[seg, rows, :], gu_w[seg])
        back = dot_nt(values[seg, rows, :], down_w[seg])
        gate_pre, up_pre = pre[:, :half], pre[:, half:]
        gate_sig = jax.nn.sigmoid(gate_pre)
        gated = gate_pre * gate_sig
        hidden[rows, :] = (gated * up_pre).astype(jnp.bfloat16)
        term[rows, pl.ds(0, half)] = (
            back * up_pre * gate_sig * (1.0 + gate_pre * (1.0 - gate_sig))
        ).astype(jnp.bfloat16)
        term[rows, pl.ds(half, half)] = (back * gated).astype(jnp.bfloat16)

    def first_terms(c):
        @pl.when(ctx == 1)
        def _():
            from_mate(c)

        terms(0, c)

    def project(c, carry):
        @pl.when(c == 0)
        def _():
            landed(1, blocks - 1, 0)

        @pl.when(c > 0)
        def _():
            landed(c * blocks, blocks, c)

        lax.fori_loop(c * blocks, (c + 1) * blocks, fill, 0)
        rows = pl.ds(c * chunk, chunk)
        x = tokens[rows, :]
        k = dot_nn(x, wk[...])
        keys[ctx, rows, :] = (k * row_scale(k)).astype(jnp.bfloat16)
        share(keys, key_send, key_recv, ctx, c).start()
        rate = dot_nn(x, rate_w[...])
        rate = jnp.maximum(rate, 0.0) + jnp.log1p(jnp.exp(-jnp.abs(rate)))
        v = dot_nn(x, wv[...])
        values[ctx, rows, :] = (rate[:, :1] * v).astype(jnp.bfloat16)
        share(values, val_send, val_recv, ctx, c).start()
        q = dot_nn(x, wq[...])
        queries[rows, :] = (q * row_scale(q)).astype(jnp.bfloat16)

        @pl.when(c > 0)
        def _():
            first_terms(c - 1)

        return carry

    lax.fori_loop(0, GROUPS, project, 0)
    first_terms(GROUPS - 1)

    def share_sums(seg):
        return pltpu.make_async_remote_copy(
            src_ref=sums.at[seg], dst_ref=other_sums.at[seg], send_sem=sum_send.at[seg], recv_sem=sum_recv.at[seg],
            device_id=mate, device_id_type=MESH)

    def share_weights(seg):
        return (
            pltpu.make_async_remote_copy(
                src_ref=gu_w.at[seg + 1], dst_ref=other_gu, send_sem=w_send.at[0], recv_sem=w_recv.at[0],
                device_id=mate, device_id_type=MESH),
            pltpu.make_async_remote_copy(
                src_ref=down_w.at[seg + 1], dst_ref=other_down, send_sem=w_send.at[1], recv_sem=w_recv.at[1],
                device_id=mate, device_id_type=MESH),
        )

    def renew(seg):
        def slopes(j, carry):
            cols = pl.ds(pl.multiple_of(j * half, 128), half)
            g = dot_tn(term[:, cols], keys[seg])
            grad[pl.ds(j * half, half), :] = g
            sums[seg, pl.ds(j, 1), :] = jnp.sum(g * g, axis=0, keepdims=True)
            return carry

        lax.fori_loop(0, 2, slopes, 0)
        share_sums(seg).start()
        grad_down[...] = dot_tn(hidden[...], values[seg])
        g = grad_down[...]
        down_w[seg + 1] = (
            down_w[seg].astype(jnp.float32) + step_size * g * row_scale(g)
        ).astype(jnp.bfloat16)
        share_sums(seg).wait_recv()
        for j in range(2):
            rows = pl.ds(j * half, half)
            total = sums[seg, pl.ds(j, 1), :] + other_sums[seg, pl.ds(j, 1), :]
            scale = step_size * lax.rsqrt(total * (1.0 / width) + 1e-06)
            gu_w[seg + 1, rows, :] = (
                gu_w[seg, rows, :].astype(jnp.float32) + grad[rows, :] * scale
            ).astype(jnp.bfloat16)

    renew(0)

    @pl.when(ctx == 1)
    def _():
        for copy in share_weights(0):
            copy.start()

    @pl.when(ctx == 0)
    def _():
        def one(c, carry):
            from_mate(c)
            return carry

        lax.fori_loop(0, GROUPS, one, 0)

    def second_terms(c, carry):
        terms(1, c)
        return carry

    lax.fori_loop(0, GROUPS, second_terms, 0)
    renew(1)

    @pl.when(ctx == 0)
    def _():
        for copy in share_weights(1):
            copy.start()

    def answer_half(rows, gu):
        pre = dot_nt(queries[rows, :], gu)
        q_gate, q_up = pre[:, :half], pre[:, half:]
        return (q_gate * jax.nn.sigmoid(q_gate) * q_up).astype(jnp.bfloat16)

    def answer_own(c, carry):
        rows = pl.ds(c * chunk, chunk)
        hidden[rows, :] = answer_half(rows, gu_w[ctx + 1])
        return carry

    lax.fori_loop(0, GROUPS, answer_own, 0)
    for copy in share_weights(0):
        copy.wait_recv()

    def out_copy(c):
        rows = pl.ds(c * chunk, chunk)
        return pltpu.make_async_copy(result.at[rows], out_ref.at[rows], load_sem.at[c])

    def answer(c, carry):
        rows = pl.ds(c * chunk, chunk)
        y = dot_nn(hidden[rows, :], down_w[ctx + 1])
        y = y + dot_nn(answer_half(rows, other_gu[...]), other_down[...])
        result[rows, :] = (y * row_scale(y) * gain[...].reshape(1, width)).astype(jnp.bfloat16)
        out_copy(c).start()
        return carry

    lax.fori_loop(0, GROUPS, answer, 0)

    def sent(c, carry):
        share(keys, key_send, key_recv, ctx, c).wait_send()
        share(values, val_send, val_recv, ctx, c).wait_send()
        out_copy(c).wait()
        return carry

    lax.fori_loop(0, GROUPS, sent, 0)
    for seg in range(2):
        share_sums(seg).wait_send()
    for copy in share_weights(0):
        copy.wait_send()
    for stage in range(3):
        for copy in stage_copies(stage, False):
            copy.wait_send()
    to_order.wait()
    piece = send.at[pl.ds(1, LANES - 1)]
    pltpu.make_async_remote_copy(
        src_ref=piece, dst_ref=piece, send_sem=send_sem, recv_sem=recv_sem.at[0],
        device_id=mate, device_id_type=MESH).wait_send()


def scene(*operands):
    width = operands[0].shape[2]
    rows = LANES * BLK
    half = width // 2
    any_ = pl.BlockSpec(memory_space=pl.ANY)
    bf, f32, i32, dma, vmem = jnp.bfloat16, jnp.float32, jnp.int32, pltpu.SemaphoreType.DMA, pltpu.VMEM
    square = vmem((width, width), bf)
    return pl.pallas_call(
        scene_kernel,
        out_shape=(jax.ShapeDtypeStruct((rows, width), bf), jax.ShapeDtypeStruct((8, 128), i32)),
        in_specs=[any_] * len(operands),
        out_specs=(any_, any_),
        scratch_shapes=[
            vmem((LANES, BLK, width), bf), vmem((1, LANES), i32), square, square, square, vmem((width,), bf),
            square, square, square, vmem((width,), f32), vmem((width, 128), bf),
            vmem((8, 128), i32), pltpu.SMEM((8, 128), i32), vmem((8, 128), i32), pltpu.SMEM((8, 128), i32),
            vmem((LANES, BLK, width), bf), vmem((LANES, BLK, width), bf),
            vmem((SIDE, SIDE, SIDE, BLK, width), bf), vmem((SIDE, SIDE, SIDE, 2, 128), i32),
            vmem((rows, width), bf), vmem((rows, width), bf),
            vmem((2, rows, width), bf), vmem((2, rows, width), bf), vmem((rows, width), bf), vmem((rows, half), bf),
            vmem((width, width), f32), vmem((half, width), f32),
            vmem((3, width, width), bf), vmem((3, half, width), bf),
            square, vmem((half, width), bf), vmem((2, 8, width), f32), vmem((2, 8, width), f32), vmem((rows, width), bf),
            dma((10,)), dma((2,)), dma, dma((GROUPS,)),
            dma((3, 3, 3)), dma((3, 3, 3)), dma((3, 3)), dma((3, 3)),
            dma((4,)), dma((4,)), dma((4,)), dma((4,)), dma((2,)), dma((2,)), dma((2,)), dma((2,)),
        ],
        compiler_params=pltpu.CompilerParams(
            collective_id=0, has_side_effects=True, vmem_limit_bytes=60 << 20
        ),
        name="scene",
    )(*operands)


def settle_kernel(order_ref, blocks_ref, out_ref, sem):
    def move(r, carry):
        code = order_ref[5, r]
        slot = jnp.where(code < LANES, code, order_ref[4, jnp.maximum(code - LANES, 0)])
        pltpu.make_async_copy(blocks_ref.at[slot], out_ref.at[r], sem).start()
        return carry

    lax.fori_loop(0, LANES, move, 0)
    pltpu.make_async_copy(blocks_ref, out_ref, sem).wait()


def settle(order, blocks):
    return pl.pallas_call(
        settle_kernel,
        out_shape=jax.ShapeDtypeStruct(blocks.shape, blocks.dtype),
        in_specs=[pl.BlockSpec(memory_space=pltpu.SMEM), pl.BlockSpec(memory_space=pltpu.VMEM)],
        out_specs=pl.BlockSpec(memory_space=pl.ANY),
        scratch_shapes=[pltpu.SemaphoreType.DMA],
        name="settle",
    )(order, blocks)


def body(view_tokens, destinations, w_query, w_key, w_value, rate_vector, fast_gate, fast_up, fast_down, out_gain):
    width = view_tokens.shape[2]
    slots, order = scene(
        view_tokens.reshape(LANES, BLK, width), destinations, w_query, w_key, w_value, rate_vector,
        fast_gate, fast_up, fast_down, out_gain
    )
    out = settle(order, slots.reshape(LANES, BLK, width))
    return out.reshape(1, LANES * BLK, width)


def solution(mesh):
    placed = (P("lane", "ctx", None), P("lane", "ctx"), P(), P(), P(), P(), P(), P(), P(), P())
    return jax.shard_map(
        body, mesh=mesh, in_specs=placed, out_specs=P("lane", "ctx", None), check_vma=False
    )
```

```python
import jax
import jax.numpy as jnp
from jax import lax
from jax.experimental import pallas as pl
from jax.experimental.pallas import tpu as pltpu
from jax.sharding import PartitionSpec as P

MESH = pl.DeviceIdType.MESH
LANES = 64
BLK = 16
SIDE = 4
GROUPS = 4
ORDERS = ((2, 1, 0), (0, 2, 1), (1, 0, 2))


def coords_of(lane):
    return (lane // 16, (lane // 4) % 4, lane % 4)


def lane_of(coords):
    return coords[0] * 16 + coords[1] * 4 + coords[2]


def dot_nn(left, right):
    return jnp.dot(left, right, preferred_element_type=jnp.float32)


def dot_nt(left, right):
    return lax.dot_general(left, right, (((1,), (1,)), ((), ())), preferred_element_type=jnp.float32)


def row_scale(values):
    return lax.rsqrt(jnp.mean(values * values, axis=-1, keepdims=True) + 1e-06)


def offset_of(k):
    dz, dy = (k // 4) % SIDE, k % SIDE
    return dz, dy, (k // 16 + 2 * SIDE - dz - dy) % SIDE


def spread(row):
    return jnp.broadcast_to(row, (128, 128)).T[:LANES]


def prefix(counts, source):
    upto = counts
    shift = 1
    while shift < LANES:
        upto = upto + jnp.where(source >= shift, pltpu.roll(upto, shift, axis=0), 0)
        shift *= 2
    return upto - counts


def send_rows(dest_row):
    block = lax.broadcasted_iota(jnp.int32, (LANES, 128), 0)
    lane = lax.broadcasted_iota(jnp.int32, (LANES, 128), 1)
    lane_row = lax.broadcasted_iota(jnp.int32, (1, 128), 1)
    named = spread(dest_row) == lane
    count = jnp.sum(named.astype(jnp.int32), axis=0, keepdims=True)
    total = jnp.sum(jnp.where(named, block, 0), axis=0, keepdims=True)
    first = jnp.min(jnp.where(named, block, LANES - 1), axis=0, keepdims=True)

    def of(mask, value):
        return jnp.sum(spread(jnp.where(mask, value, 0)), axis=0, keepdims=True)

    twice = count == 2
    absent = (count == 0) & (lane_row < LANES)
    return first, of(twice, total - first), of(twice, lane_row), of(absent, lane_row)


def order_rows(doubled, missed, me):
    source = lax.broadcasted_iota(jnp.int32, (LANES, 128), 0)
    spot = lax.broadcasted_iota(jnp.int32, (LANES, 128), 1)
    usual = (missed != me).astype(jnp.int32)
    hole = 1 - usual
    double = (doubled == me).astype(jnp.int32)
    start = prefix(usual + double, source)
    hole_rank = prefix(hole, source)
    double_rank = prefix(double, source)
    dz, dy, dx = (me // 16 - source // 16) % SIDE, (me // 4 - source // 4) % SIDE, (me - source) % SIDE
    slot = ((dz + dy + dx) % SIDE) * 16 + dz * 4 + dy

    def row(mask, value):
        return jnp.sum(jnp.where(mask, value, 0), axis=0, keepdims=True)

    by_source = row(source == spot, hole_rank)
    filler = (double == 1) & (double_rank == by_source)
    return (
        row(source == spot, usual),
        row(filler, source // 16),
        row(filler, (source // 4) % SIDE),
        row(filler, source % SIDE),
        row((hole == 1) & (hole_rank == spot), slot),
        row((usual == 1) & (start == spot), slot)
        + row((double == 1) & (start + usual == spot), double_rank + LANES),
    )


def scene_kernel(view_hbm, dest_hbm, wq_hbm, wk_hbm, wv_hbm, rate_hbm, gate_hbm, up_hbm, down_hbm, gain_hbm,
                 out_ref, order_ref,
                 view, dest, wq, wk, wv, rate_row, gate, up, down, gain, rate_w,
                 idx_v, idx_s, rows_v, rows_s, send, prim, ext, metas,
                 tokens, queries, keys, values, term, hidden, asked, grad, grad_down, gu_w, down_w,
                 other_gu, other_down, sums, other_sums, result,
                 load_sem, local_sem, send_sem, recv_sem, ext_send, ext_recv, meta_send, meta_recv,
                 key_send, key_recv, val_send, val_recv, sum_send, sum_recv, w_send, w_recv):
    me = lax.axis_index("lane")
    ctx = lax.axis_index("ctx")
    here = coords_of(me)
    mate = (me, 1 - ctx)
    width = tokens.shape[1]
    half = width // 2
    part = width // 3
    chunk = tokens.shape[0] // GROUPS
    blocks = chunk // BLK
    step_size = 0.5 * width ** (-0.5)

    barrier = pltpu.get_barrier_semaphore()

    def greet(k, carry):
        pl.semaphore_signal(barrier, inc=1, device_id=(lax.rem(me + k, LANES), ctx), device_id_type=MESH)
        return carry

    lax.fori_loop(1, LANES, greet, 0)
    pl.semaphore_signal(barrier, inc=1, device_id=mate, device_id_type=MESH)

    loads = [
        pltpu.make_async_copy(a, b, load_sem.at[i])
        for i, (a, b) in enumerate((
            (dest_hbm, dest), (view_hbm, view), (wk_hbm, wk), (wv_hbm, wv), (wq_hbm, wq), (gate_hbm, gate),
            (up_hbm, up), (down_hbm, down), (rate_hbm, rate_row), (gain_hbm, gain)))
    ]
    for copy in loads:
        copy.start()
    loads[0].wait()

    first, second, doubled, missed = send_rows(jnp.concatenate([dest[...], dest[...]], axis=1))
    idx_v[0:1, :] = first
    idx_v[1:2, :] = second
    metas[here[0], here[1], here[2], 0:1, :] = doubled
    metas[here[0], here[1], here[2], 1:2, :] = missed
    to_idx = pltpu.make_async_copy(idx_v, idx_s, local_sem.at[0])
    to_idx.start()
    to_idx.wait()
    loads[1].wait()

    def block_of(b):
        return view[b]

    def peer(k):
        d = offset_of(k)
        return lane_of([(h + o) % SIDE for h, o in zip(here, d)])

    ext[here[0], here[1], here[2]] = block_of(idx_s[1, 0])
    prim[0] = block_of(idx_s[0, me])

    def pack(k, carry):
        send[k] = block_of(idx_s[0, peer(k)])
        return carry

    lax.fori_loop(1, LANES, pack, 0)
    pl.semaphore_wait(barrier, LANES)

    def stage_copy(ref, tail, order, stage, delta, back, sends, recvs):
        axis = order[stage]
        spot = list(here)
        if back:
            spot[axis] = (here[axis] - delta) % SIDE
        for done in order[:stage]:
            spot[done] = pl.ds(0, SIDE)
        to = list(here)
        to[axis] = (here[axis] + delta) % SIDE
        slab = ref.at[(*spot, *tail)]
        return pltpu.make_async_remote_copy(
            src_ref=slab, dst_ref=slab, send_sem=sends, recv_sem=recvs,
            device_id=(lane_of(to), ctx), device_id_type=MESH)

    def stage_copies(stage, back):
        made = []
        for delta in (1, 3, 2):
            made.append(stage_copy(
                metas, (), ORDERS[0], stage, delta, back,
                meta_send.at[stage, delta - 1], meta_recv.at[stage, delta - 1]))
            for p in range(3):
                made.append(stage_copy(
                    ext, (slice(None), pl.ds(p * part, part)), ORDERS[p], stage, delta, back,
                    ext_send.at[p, stage, delta - 1], ext_recv.at[p, stage, delta - 1]))
        return made

    def start_stage(stage):
        for copy in stage_copies(stage, False):
            copy.start()

    def end_stage(stage):
        for copy in stage_copies(stage, True):
            copy.wait_recv()

    def post(k, carry):
        pltpu.make_async_remote_copy(
            src_ref=send.at[k], dst_ref=prim.at[k],
            send_sem=send_sem, recv_sem=recv_sem.at[k // blocks],
            device_id=(peer(k), ctx), device_id_type=MESH).start()
        return carry

    start_stage(0)
    lax.fori_loop(1, blocks, post, 0)
    end_stage(0)
    start_stage(1)
    end_stage(1)
    start_stage(2)
    for copy in loads[2:]:
        copy.wait()
    mine = pl.ds(pl.multiple_of(ctx * half, 128), half)
    gu_w[0, pl.ds(0, half), :] = gate[:, mine].T
    gu_w[0, pl.ds(half, half), :] = up[:, mine].T
    down_w[0] = down[mine, :]
    rate_w[...] = jnp.broadcast_to(rate_row[...].astype(jnp.float32).reshape(1, width), (128, width)).T.astype(jnp.bfloat16)
    end_stage(2)
    lax.fori_loop(blocks, LANES, post, 0)
    table = metas[...].reshape(LANES, 2, 128)
    for i, row in enumerate(order_rows(table[:, 0, :], table[:, 1, :], me)):
        rows_v[i:i + 1, :] = row
    to_rows = pltpu.make_async_copy(rows_v, rows_s, local_sem.at[0])
    to_rows.start()
    to_order = pltpu.make_async_copy(rows_v, order_ref, local_sem.at[1])
    to_order.start()
    to_rows.wait()

    def share(ref, sends, recvs, seg, c):
        piece = ref.at[seg, pl.ds(c * chunk, chunk)]
        return pltpu.make_async_remote_copy(
            src_ref=piece, dst_ref=piece, send_sem=sends.at[c], recv_sem=recvs.at[c],
            device_id=mate, device_id_type=MESH)

    def fill(k, carry):
        d = offset_of(k)
        s = lane_of([(h - o) % SIDE for h, o in zip(here, d)])
        keep = rows_s[0, s].astype(jnp.float32)
        doubled_block = ext[rows_s[1, s], rows_s[2, s], rows_s[3, s]].astype(jnp.float32)
        block = prim[k].astype(jnp.float32) * keep + doubled_block * (1.0 - keep)
        tokens[pl.ds(pl.multiple_of(k * BLK, BLK), BLK), :] = block.astype(jnp.bfloat16)
        return carry

    def landed(lo, count, g):
        piece = prim.at[pl.ds(lo, count)]
        pltpu.make_async_remote_copy(
            src_ref=piece, dst_ref=piece, send_sem=send_sem, recv_sem=recv_sem.at[g],
            device_id=mate, device_id_type=MESH).wait_recv()

    def from_mate(c):
        share(keys, key_send, key_recv, 1 - ctx, c).wait_recv()
        share(values, val_send, val_recv, 1 - ctx, c).wait_recv()

    def terms(seg, c):
        rows = pl.ds(pl.multiple_of(c * chunk, chunk), chunk)
        pre = dot_nt(gu_w[seg], keys[seg, rows, :])
        back = dot_nt(down_w[seg], values[seg, rows, :])
        gate_pre, up_pre = pre[:half], pre[half:]
        gate_sig = jax.nn.sigmoid(gate_pre)
        gated = gate_pre * gate_sig
        hidden[:, rows] = (gated * up_pre).astype(jnp.bfloat16)
        term[pl.ds(0, half), rows] = (
            back * up_pre * gate_sig * (1.0 + gate_pre * (1.0 - gate_sig))
        ).astype(jnp.bfloat16)
        term[pl.ds(half, half), rows] = (back * gated).astype(jnp.bfloat16)

    def first_terms(c):
        @pl.when(ctx == 1)
        def _():
            from_mate(c)

        terms(0, c)

    def project(c, carry):
        @pl.when(c == 0)
        def _():
            landed(1, blocks - 1, 0)

        @pl.when(c > 0)
        def _():
            landed(c * blocks, blocks, c)

        lax.fori_loop(0, blocks, lambda j, carry: fill(c * blocks + j, carry), 0, unroll=4)
        rows = pl.ds(c * chunk, chunk)
        x = tokens[rows, :]
        k = dot_nn(x, wk[...])
        keys[ctx, rows, :] = (k * row_scale(k)).astype(jnp.bfloat16)
        share(keys, key_send, key_recv, ctx, c).start()
        rate = dot_nn(x, rate_w[...])
        rate = jnp.maximum(rate, 0.0) + jnp.log1p(jnp.exp(-jnp.abs(rate)))
        v = dot_nn(x, wv[...])
        values[ctx, rows, :] = (rate[:, :1] * v).astype(jnp.bfloat16)
        share(values, val_send, val_recv, ctx, c).start()
        q = dot_nn(x, wq[...])
        queries[rows, :] = (q * row_scale(q)).astype(jnp.bfloat16)

        @pl.when(c > 0)
        def _():
            first_terms(c - 1)

        return carry

    lax.fori_loop(0, GROUPS, project, 0)
    first_terms(GROUPS - 1)

    def share_sums(seg):
        return pltpu.make_async_remote_copy(
            src_ref=sums.at[seg], dst_ref=other_sums.at[seg], send_sem=sum_send.at[seg], recv_sem=sum_recv.at[seg],
            device_id=mate, device_id_type=MESH)

    def share_weights(seg, which=(0, 1, 2)):
        made = []
        for i in which:
            rows = pl.ds(i * half, half)
            source, target = (
                (down_w.at[seg + 1], other_down) if i == 2 else (gu_w.at[seg + 1, rows], other_gu.at[rows]))
            made.append(pltpu.make_async_remote_copy(
                src_ref=source, dst_ref=target, send_sem=w_send.at[i], recv_sem=w_recv.at[i],
                device_id=mate, device_id_type=MESH))
        return made

    def send_weights(seg, i):
        @pl.when(ctx == 1 - seg)
        def _():
            share_weights(seg, (i,))[0].start()

    def renew(seg):
        def slopes(j, carry):
            units = pl.ds(pl.multiple_of(j * half, 128), half)
            g = dot_nn(term[units, :], keys[seg])
            grad[units, :] = g
            sums[seg, pl.ds(j, 1), :] = jnp.sum(g * g, axis=0, keepdims=True)
            return carry

        lax.fori_loop(0, 2, slopes, 0)
        share_sums(seg).start()
        grad_down[...] = dot_nn(hidden[...], values[seg])
        g = grad_down[...]
        down_w[seg + 1] = (
            down_w[seg].astype(jnp.float32) + step_size * g * row_scale(g)
        ).astype(jnp.bfloat16)
        send_weights(seg, 2)
        share_sums(seg).wait_recv()
        for j in range(2):
            rows = pl.ds(j * half, half)
            total = sums[seg, pl.ds(j, 1), :] + other_sums[seg, pl.ds(j, 1), :]
            scale = step_size * lax.rsqrt(total * (1.0 / width) + 1e-06)
            gu_w[seg + 1, rows, :] = (
                gu_w[seg, rows, :].astype(jnp.float32) + grad[rows, :] * scale
            ).astype(jnp.bfloat16)
            send_weights(seg, j)

    renew(0)

    @pl.when(ctx == 0)
    def _():
        def one(c, carry):
            from_mate(c)
            return carry

        lax.fori_loop(0, GROUPS, one, 0)

    def second_terms(c, carry):
        terms(1, c)
        return carry

    lax.fori_loop(0, GROUPS, second_terms, 0)
    renew(1)

    def answer_half(rows, gu):
        pre = dot_nt(queries[rows, :], gu)
        q_gate, q_up = pre[:, :half], pre[:, half:]
        return (q_gate * jax.nn.sigmoid(q_gate) * q_up).astype(jnp.bfloat16)

    def answer_own(c, carry):
        rows = pl.ds(c * chunk, chunk)
        asked[rows, :] = answer_half(rows, gu_w[ctx + 1])
        return carry

    lax.fori_loop(0, GROUPS, answer_own, 0)
    for copy in share_weights(0):
        copy.wait_recv()

    def out_copy(c):
        rows = pl.ds(c * chunk, chunk)
        return pltpu.make_async_copy(result.at[rows], out_ref.at[rows], load_sem.at[c])

    def answer(c, carry):
        rows = pl.ds(c * chunk, chunk)
        y = dot_nn(asked[rows, :], down_w[ctx + 1])
        y = y + dot_nn(answer_half(rows, other_gu[...]), other_down[...])
        result[rows, :] = (y * row_scale(y) * gain[...].reshape(1, width)).astype(jnp.bfloat16)
        out_copy(c).start()
        return carry

    lax.fori_loop(0, GROUPS, answer, 0)

    def sent(c, carry):
        share(keys, key_send, key_recv, ctx, c).wait_send()
        share(values, val_send, val_recv, ctx, c).wait_send()
        out_copy(c).wait()
        return carry

    lax.fori_loop(0, GROUPS, sent, 0)
    for seg in range(2):
        share_sums(seg).wait_send()
    for copy in share_weights(0):
        copy.wait_send()
    for stage in range(3):
        for copy in stage_copies(stage, False):
            copy.wait_send()
    to_order.wait()
    piece = send.at[pl.ds(1, LANES - 1)]
    pltpu.make_async_remote_copy(
        src_ref=piece, dst_ref=piece, send_sem=send_sem, recv_sem=recv_sem.at[0],
        device_id=mate, device_id_type=MESH).wait_send()


def scene(*operands):
    width = operands[0].shape[2]
    rows = LANES * BLK
    half = width // 2
    any_ = pl.BlockSpec(memory_space=pl.ANY)
    bf, f32, i32, dma, vmem = jnp.bfloat16, jnp.float32, jnp.int32, pltpu.SemaphoreType.DMA, pltpu.VMEM
    square = vmem((width, width), bf)
    return pl.pallas_call(
        scene_kernel,
        out_shape=(jax.ShapeDtypeStruct((rows, width), bf), jax.ShapeDtypeStruct((8, 128), i32)),
        in_specs=[any_] * len(operands),
        out_specs=(any_, any_),
        scratch_shapes=[
            vmem((LANES, BLK, width), bf), vmem((1, LANES), i32), square, square, square, vmem((width,), bf),
            square, square, square, vmem((width,), f32), vmem((width, 128), bf),
            vmem((8, 128), i32), pltpu.SMEM((8, 128), i32), vmem((8, 128), i32), pltpu.SMEM((8, 128), i32),
            vmem((LANES, BLK, width), bf), vmem((LANES, BLK, width), bf),
            vmem((SIDE, SIDE, SIDE, BLK, width), bf), vmem((SIDE, SIDE, SIDE, 2, 128), i32),
            vmem((rows, width), bf), vmem((rows, width), bf),
            vmem((2, rows, width), bf), vmem((2, rows, width), bf), vmem((width, rows), bf), vmem((half, rows), bf),
            vmem((rows, half), bf),
            vmem((width, width), f32), vmem((half, width), f32),
            vmem((3, width, width), bf), vmem((3, half, width), bf),
            square, vmem((half, width), bf), vmem((2, 8, width), f32), vmem((2, 8, width), f32), vmem((rows, width), bf),
            dma((10,)), dma((2,)), dma, dma((GROUPS,)),
            dma((3, 3, 3)), dma((3, 3, 3)), dma((3, 3)), dma((3, 3)),
            dma((4,)), dma((4,)), dma((4,)), dma((4,)), dma((2,)), dma((2,)), dma((3,)), dma((3,)),
        ],
        compiler_params=pltpu.CompilerParams(
            collective_id=0, has_side_effects=True, vmem_limit_bytes=60 << 20
        ),
        name="scene",
    )(*operands)


def settle_kernel(order_ref, blocks_ref, out_ref, sem):
    def move(r, carry):
        code = order_ref[5, r]
        slot = jnp.where(code < LANES, code, order_ref[4, jnp.maximum(code - LANES, 0)])
        pltpu.make_async_copy(blocks_ref.at[slot], out_ref.at[r], sem).start()
        return carry

    lax.fori_loop(0, LANES, move, 0)
    pltpu.make_async_copy(blocks_ref, out_ref, sem).wait()


def settle(order, blocks):
    return pl.pallas_call(
        settle_kernel,
        out_shape=jax.ShapeDtypeStruct(blocks.shape, blocks.dtype),
        in_specs=[pl.BlockSpec(memory_space=pltpu.SMEM), pl.BlockSpec(memory_space=pltpu.VMEM)],
        out_specs=pl.BlockSpec(memory_space=pl.ANY),
        scratch_shapes=[pltpu.SemaphoreType.DMA],
        name="settle",
    )(order, blocks)


def body(view_tokens, destinations, w_query, w_key, w_value, rate_vector, fast_gate, fast_up, fast_down, out_gain):
    width = view_tokens.shape[2]
    slots, order = scene(
        view_tokens.reshape(LANES, BLK, width), destinations, w_query, w_key, w_value, rate_vector,
        fast_gate, fast_up, fast_down, out_gain
    )
    out = settle(order, slots.reshape(LANES, BLK, width))
    return out.reshape(1, LANES * BLK, width)


def solution(mesh):
    placed = (P("lane", "ctx", None), P("lane", "ctx"), P(), P(), P(), P(), P(), P(), P(), P())
    return jax.shard_map(
        body, mesh=mesh, in_specs=placed, out_specs=P("lane", "ctx", None), check_vma=False
    )
```

```python
import jax
import jax.numpy as jnp
from jax import lax
from jax.experimental import pallas as pl
from jax.experimental.pallas import tpu as pltpu
from jax.sharding import PartitionSpec as P

MESH = pl.DeviceIdType.MESH
LANES = 64
BLK = 16
SIDE = 4
GROUPS = 4
ORDERS = ((2, 1, 0), (0, 2, 1), (1, 0, 2))


def coords_of(lane):
    return (lane // 16, (lane // 4) % 4, lane % 4)


def lane_of(coords):
    return coords[0] * 16 + coords[1] * 4 + coords[2]


def dot_nn(left, right):
    return jnp.dot(left, right, preferred_element_type=jnp.float32)


def dot_nt(left, right):
    return lax.dot_general(left, right, (((1,), (1,)), ((), ())), preferred_element_type=jnp.float32)


def row_scale(values):
    return lax.rsqrt(jnp.mean(values * values, axis=-1, keepdims=True) + 1e-06)


def offset_of(k):
    dz, dy = (k // 4) % SIDE, k % SIDE
    return dz, dy, (k // 16 + 2 * SIDE - dz - dy) % SIDE


def spread(row):
    return jnp.broadcast_to(row, (128, 128)).T[:LANES]


def prefix(counts, source):
    upto = counts
    shift = 1
    while shift < LANES:
        upto = upto + jnp.where(source >= shift, pltpu.roll(upto, shift, axis=0), 0)
        shift *= 2
    return upto - counts


def send_rows(dest_row):
    block = lax.broadcasted_iota(jnp.int32, (LANES, 128), 0)
    lane = lax.broadcasted_iota(jnp.int32, (LANES, 128), 1)
    lane_row = lax.broadcasted_iota(jnp.int32, (1, 128), 1)
    named = spread(dest_row) == lane
    count = jnp.sum(named.astype(jnp.int32), axis=0, keepdims=True)
    total = jnp.sum(jnp.where(named, block, 0), axis=0, keepdims=True)
    first = jnp.min(jnp.where(named, block, LANES - 1), axis=0, keepdims=True)

    def of(mask, value):
        return jnp.sum(spread(jnp.where(mask, value, 0)), axis=0, keepdims=True)

    twice = count == 2
    absent = (count == 0) & (lane_row < LANES)
    return first, of(twice, total - first), of(twice, lane_row), of(absent, lane_row)


def order_rows(doubled, missed, me):
    source = lax.broadcasted_iota(jnp.int32, (LANES, 128), 0)
    spot = lax.broadcasted_iota(jnp.int32, (LANES, 128), 1)
    usual = (missed != me).astype(jnp.int32)
    hole = 1 - usual
    double = (doubled == me).astype(jnp.int32)
    start = prefix(usual + double, source)
    hole_rank = prefix(hole, source)
    double_rank = prefix(double, source)
    dz, dy, dx = (me // 16 - source // 16) % SIDE, (me // 4 - source // 4) % SIDE, (me - source) % SIDE
    slot = ((dz + dy + dx) % SIDE) * 16 + dz * 4 + dy

    def row(mask, value):
        return jnp.sum(jnp.where(mask, value, 0), axis=0, keepdims=True)

    by_source = row(source == spot, hole_rank)
    filler = (double == 1) & (double_rank == by_source)
    return (
        row(source == spot, usual),
        row(filler, source // 16),
        row(filler, (source // 4) % SIDE),
        row(filler, source % SIDE),
        row((hole == 1) & (hole_rank == spot), slot),
        row((usual == 1) & (start == spot), slot)
        + row((double == 1) & (start + usual == spot), double_rank + LANES),
    )


def scene_kernel(view_hbm, dest_hbm, wq_hbm, wk_hbm, wv_hbm, rate_hbm, gate_hbm, up_hbm, down_hbm, gain_hbm,
                 out_ref, order_ref,
                 view, dest, wq, wk, wv, rate_row, gate, up, down, gain, rate_w,
                 idx_v, idx_s, rows_v, rows_s, send, prim, ext, metas,
                 tokens, queries, keys, values, term, hidden, asked, grad, grad_down, gu_w, down_w,
                 other_gu, other_down, sums, other_sums, result,
                 load_sem, local_sem, send_sem, recv_sem, ext_send, ext_recv, meta_send, meta_recv,
                 key_send, key_recv, val_send, val_recv, sum_send, sum_recv, w_send, w_recv):
    me = lax.axis_index("lane")
    ctx = lax.axis_index("ctx")
    here = coords_of(me)
    mate = (me, 1 - ctx)
    width = tokens.shape[1]
    half = width // 2
    part = width // 3
    chunk = tokens.shape[0] // GROUPS
    blocks = chunk // BLK
    step_size = 0.5 * width ** (-0.5)

    barrier = pltpu.get_barrier_semaphore()

    def greet(k, carry):
        pl.semaphore_signal(barrier, inc=1, device_id=(lax.rem(me + k, LANES), ctx), device_id_type=MESH)
        return carry

    lax.fori_loop(1, LANES, greet, 0)
    pl.semaphore_signal(barrier, inc=1, device_id=mate, device_id_type=MESH)

    loads = [
        pltpu.make_async_copy(a, b, load_sem.at[i])
        for i, (a, b) in enumerate((
            (dest_hbm, dest), (view_hbm, view), (wk_hbm, wk), (wv_hbm, wv), (wq_hbm, wq), (gate_hbm, gate),
            (up_hbm, up), (down_hbm, down), (rate_hbm, rate_row), (gain_hbm, gain)))
    ]
    for copy in loads:
        copy.start()
    loads[0].wait()

    first, second, doubled, missed = send_rows(jnp.concatenate([dest[...], dest[...]], axis=1))
    idx_v[0:1, :] = first
    idx_v[1:2, :] = second
    metas[here[0], here[1], here[2], 0:1, :] = doubled
    metas[here[0], here[1], here[2], 1:2, :] = missed
    to_idx = pltpu.make_async_copy(idx_v, idx_s, local_sem.at[0])
    to_idx.start()
    to_idx.wait()
    loads[1].wait()

    def block_of(b):
        return view[b]

    def peer(k):
        d = offset_of(k)
        return lane_of([(h + o) % SIDE for h, o in zip(here, d)])

    ext[here[0], here[1], here[2]] = block_of(idx_s[1, 0])
    prim[0] = block_of(idx_s[0, me])

    def pack(k, carry):
        send[k] = block_of(idx_s[0, peer(k)])
        return carry

    lax.fori_loop(1, LANES, pack, 0)
    pl.semaphore_wait(barrier, LANES)

    def stage_copy(ref, tail, order, stage, delta, back, sends, recvs):
        axis = order[stage]
        spot = list(here)
        if back:
            spot[axis] = (here[axis] - delta) % SIDE
        for done in order[:stage]:
            spot[done] = pl.ds(0, SIDE)
        to = list(here)
        to[axis] = (here[axis] + delta) % SIDE
        slab = ref.at[(*spot, *tail)]
        return pltpu.make_async_remote_copy(
            src_ref=slab, dst_ref=slab, send_sem=sends, recv_sem=recvs,
            device_id=(lane_of(to), ctx), device_id_type=MESH)

    def stage_copies(stage, back):
        made = []
        for delta in (1, 3, 2):
            made.append(stage_copy(
                metas, (), ORDERS[0], stage, delta, back,
                meta_send.at[stage, delta - 1], meta_recv.at[stage, delta - 1]))
            for p in range(3):
                made.append(stage_copy(
                    ext, (slice(None), pl.ds(p * part, part)), ORDERS[p], stage, delta, back,
                    ext_send.at[p, stage, delta - 1], ext_recv.at[p, stage, delta - 1]))
        return made

    def start_stage(stage):
        for copy in stage_copies(stage, False):
            copy.start()

    def end_stage(stage):
        for copy in stage_copies(stage, True):
            copy.wait_recv()

    def post(k, carry):
        pltpu.make_async_remote_copy(
            src_ref=send.at[k], dst_ref=prim.at[k],
            send_sem=send_sem, recv_sem=recv_sem.at[k // blocks],
            device_id=(peer(k), ctx), device_id_type=MESH).start()
        return carry

    start_stage(0)
    lax.fori_loop(1, blocks, post, 0)
    end_stage(0)
    start_stage(1)
    end_stage(1)
    start_stage(2)
    for copy in loads[2:]:
        copy.wait()
    mine = pl.ds(pl.multiple_of(ctx * half, 128), half)
    gu_w[0, pl.ds(0, half), :] = gate[:, mine].T
    gu_w[0, pl.ds(half, half), :] = up[:, mine].T
    down_w[0] = down[mine, :]
    rate_w[...] = jnp.broadcast_to(rate_row[...].astype(jnp.float32).reshape(1, width), (128, width)).T.astype(jnp.bfloat16)
    end_stage(2)
    lax.fori_loop(blocks, LANES, post, 0)
    table = metas[...].reshape(LANES, 2, 128)
    for i, row in enumerate(order_rows(table[:, 0, :], table[:, 1, :], me)):
        rows_v[i:i + 1, :] = row
    to_rows = pltpu.make_async_copy(rows_v, rows_s, local_sem.at[0])
    to_rows.start()
    to_order = pltpu.make_async_copy(rows_v, order_ref, local_sem.at[1])
    to_order.start()
    to_rows.wait()

    def share(ref, sends, recvs, seg, c):
        piece = ref.at[seg, pl.ds(c * chunk, chunk)]
        return pltpu.make_async_remote_copy(
            src_ref=piece, dst_ref=piece, send_sem=sends.at[c], recv_sem=recvs.at[c],
            device_id=mate, device_id_type=MESH)

    def fill(k, carry):
        d = offset_of(k)
        s = lane_of([(h - o) % SIDE for h, o in zip(here, d)])
        keep = rows_s[0, s].astype(jnp.float32)
        doubled_block = ext[rows_s[1, s], rows_s[2, s], rows_s[3, s]].astype(jnp.float32)
        block = prim[k].astype(jnp.float32) * keep + doubled_block * (1.0 - keep)
        tokens[pl.ds(pl.multiple_of(k * BLK, BLK), BLK), :] = block.astype(jnp.bfloat16)
        return carry

    def landed(lo, count, g):
        piece = prim.at[pl.ds(lo, count)]
        pltpu.make_async_remote_copy(
            src_ref=piece, dst_ref=piece, send_sem=send_sem, recv_sem=recv_sem.at[g],
            device_id=mate, device_id_type=MESH).wait_recv()

    def from_mate(c):
        share(keys, key_send, key_recv, 1 - ctx, c).wait_recv()
        share(values, val_send, val_recv, 1 - ctx, c).wait_recv()

    def terms(seg, c):
        rows = pl.ds(pl.multiple_of(c * chunk, chunk), chunk)
        pre = dot_nt(gu_w[seg], keys[seg, rows, :])
        back = dot_nt(down_w[seg], values[seg, rows, :])
        gate_pre, up_pre = pre[:half], pre[half:]
        gate_sig = jax.nn.sigmoid(gate_pre)
        gated = gate_pre * gate_sig
        hidden[:, rows] = (gated * up_pre).astype(jnp.bfloat16)
        term[pl.ds(0, half), rows] = (
            back * up_pre * gate_sig * (1.0 + gate_pre * (1.0 - gate_sig))
        ).astype(jnp.bfloat16)
        term[pl.ds(half, half), rows] = (back * gated).astype(jnp.bfloat16)

    def first_terms(c):
        @pl.when(ctx == 1)
        def _():
            from_mate(c)

        terms(0, c)

    def project(c, carry):
        @pl.when(c == 0)
        def _():
            landed(1, blocks - 1, 0)

        @pl.when(c > 0)
        def _():
            landed(c * blocks, blocks, c)

        lax.fori_loop(0, blocks, lambda j, carry: fill(c * blocks + j, carry), 0, unroll=16)
        rows = pl.ds(c * chunk, chunk)
        x = tokens[rows, :]
        k = dot_nn(x, wk[...])
        keys[ctx, rows, :] = (k * row_scale(k)).astype(jnp.bfloat16)
        share(keys, key_send, key_recv, ctx, c).start()
        rate = dot_nn(x, rate_w[...])
        rate = jnp.maximum(rate, 0.0) + jnp.log1p(jnp.exp(-jnp.abs(rate)))
        v = dot_nn(x, wv[...])
        values[ctx, rows, :] = (rate[:, :1] * v).astype(jnp.bfloat16)
        share(values, val_send, val_recv, ctx, c).start()
        q = dot_nn(x, wq[...])
        queries[rows, :] = (q * row_scale(q)).astype(jnp.bfloat16)

        @pl.when(c > 0)
        def _():
            first_terms(c - 1)

        return carry

    lax.fori_loop(0, GROUPS, project, 0)
    first_terms(GROUPS - 1)

    def share_sums(seg):
        return pltpu.make_async_remote_copy(
            src_ref=sums.at[seg], dst_ref=other_sums.at[seg], send_sem=sum_send.at[seg], recv_sem=sum_recv.at[seg],
            device_id=mate, device_id_type=MESH)

    def share_weights(seg, which=(0, 1, 2)):
        made = []
        for i in which:
            rows = pl.ds(i * half, half)
            source, target = (
                (down_w.at[seg + 1], other_down) if i == 2 else (gu_w.at[seg + 1, rows], other_gu.at[rows]))
            made.append(pltpu.make_async_remote_copy(
                src_ref=source, dst_ref=target, send_sem=w_send.at[i], recv_sem=w_recv.at[i],
                device_id=mate, device_id_type=MESH))
        return made

    def send_weights(seg, i):
        @pl.when(ctx == 1 - seg)
        def _():
            share_weights(seg, (i,))[0].start()

    def renew(seg):
        def slopes(j, carry):
            units = pl.ds(pl.multiple_of(j * half, 128), half)
            g = dot_nn(term[units, :], keys[seg])
            grad[units, :] = g
            sums[seg, pl.ds(j, 1), :] = jnp.sum(g * g, axis=0, keepdims=True)
            return carry

        lax.fori_loop(0, 2, slopes, 0)
        share_sums(seg).start()
        grad_down[...] = dot_nn(hidden[...], values[seg])
        g = grad_down[...]
        down_w[seg + 1] = (
            down_w[seg].astype(jnp.float32) + step_size * g * row_scale(g)
        ).astype(jnp.bfloat16)
        send_weights(seg, 2)
        share_sums(seg).wait_recv()
        for j in range(2):
            rows = pl.ds(j * half, half)
            total = sums[seg, pl.ds(j, 1), :] + other_sums[seg, pl.ds(j, 1), :]
            scale = step_size * lax.rsqrt(total * (1.0 / width) + 1e-06)
            gu_w[seg + 1, rows, :] = (
                gu_w[seg, rows, :].astype(jnp.float32) + grad[rows, :] * scale
            ).astype(jnp.bfloat16)
            send_weights(seg, j)

    renew(0)

    @pl.when(ctx == 0)
    def _():
        def one(c, carry):
            from_mate(c)
            return carry

        lax.fori_loop(0, GROUPS, one, 0)

    def second_terms(c, carry):
        terms(1, 2 * c)
        terms(1, 2 * c + 1)
        return carry

    lax.fori_loop(0, GROUPS // 2, second_terms, 0)
    renew(1)

    def answer_half(rows, gu):
        pre = dot_nt(queries[rows, :], gu)
        q_gate, q_up = pre[:, :half], pre[:, half:]
        return (q_gate * jax.nn.sigmoid(q_gate) * q_up).astype(jnp.bfloat16)

    def answer_own(c, carry):
        for i in range(2):
            rows = pl.ds((2 * c + i) * chunk, chunk)
            asked[rows, :] = answer_half(rows, gu_w[ctx + 1])
        return carry

    lax.fori_loop(0, GROUPS // 2, answer_own, 0)
    for copy in share_weights(0):
        copy.wait_recv()

    def out_copy(c):
        rows = pl.ds(c * chunk, chunk)
        return pltpu.make_async_copy(result.at[rows], out_ref.at[rows], load_sem.at[c])

    def answer(c, carry):
        rows = pl.ds(c * chunk, chunk)
        y = dot_nn(asked[rows, :], down_w[ctx + 1])
        y = y + dot_nn(answer_half(rows, other_gu[...]), other_down[...])
        result[rows, :] = (y * row_scale(y) * gain[...].reshape(1, width)).astype(jnp.bfloat16)
        out_copy(c).start()
        return carry

    lax.fori_loop(0, GROUPS, answer, 0)

    def sent(c, carry):
        share(keys, key_send, key_recv, ctx, c).wait_send()
        share(values, val_send, val_recv, ctx, c).wait_send()
        out_copy(c).wait()
        return carry

    lax.fori_loop(0, GROUPS, sent, 0)
    for seg in range(2):
        share_sums(seg).wait_send()
    for copy in share_weights(0):
        copy.wait_send()
    for stage in range(3):
        for copy in stage_copies(stage, False):
            copy.wait_send()
    to_order.wait()
    piece = send.at[pl.ds(1, LANES - 1)]
    pltpu.make_async_remote_copy(
        src_ref=piece, dst_ref=piece, send_sem=send_sem, recv_sem=recv_sem.at[0],
        device_id=mate, device_id_type=MESH).wait_send()


def scene(*operands):
    width = operands[0].shape[2]
    rows = LANES * BLK
    half = width // 2
    any_ = pl.BlockSpec(memory_space=pl.ANY)
    bf, f32, i32, dma, vmem = jnp.bfloat16, jnp.float32, jnp.int32, pltpu.SemaphoreType.DMA, pltpu.VMEM
    square = vmem((width, width), bf)
    return pl.pallas_call(
        scene_kernel,
        out_shape=(jax.ShapeDtypeStruct((rows, width), bf), jax.ShapeDtypeStruct((8, 128), i32)),
        in_specs=[any_] * len(operands),
        out_specs=(any_, any_),
        scratch_shapes=[
            vmem((LANES, BLK, width), bf), vmem((1, LANES), i32), square, square, square, vmem((width,), bf),
            square, square, square, vmem((width,), f32), vmem((width, 128), bf),
            vmem((8, 128), i32), pltpu.SMEM((8, 128), i32), vmem((8, 128), i32), pltpu.SMEM((8, 128), i32),
            vmem((LANES, BLK, width), bf), vmem((LANES, BLK, width), bf),
            vmem((SIDE, SIDE, SIDE, BLK, width), bf), vmem((SIDE, SIDE, SIDE, 2, 128), i32),
            vmem((rows, width), bf), vmem((rows, width), bf),
            vmem((2, rows, width), bf), vmem((2, rows, width), bf), vmem((width, rows), bf), vmem((half, rows), bf),
            vmem((rows, half), bf),
            vmem((width, width), f32), vmem((half, width), f32),
            vmem((3, width, width), bf), vmem((3, half, width), bf),
            square, vmem((half, width), bf), vmem((2, 8, width), f32), vmem((2, 8, width), f32), vmem((rows, width), bf),
            dma((10,)), dma((2,)), dma, dma((GROUPS,)),
            dma((3, 3, 3)), dma((3, 3, 3)), dma((3, 3)), dma((3, 3)),
            dma((4,)), dma((4,)), dma((4,)), dma((4,)), dma((2,)), dma((2,)), dma((3,)), dma((3,)),
        ],
        compiler_params=pltpu.CompilerParams(
            collective_id=0, has_side_effects=True, vmem_limit_bytes=60 << 20
        ),
        name="scene",
    )(*operands)


def settle_kernel(order_ref, blocks_ref, out_ref, sem):
    def move(r, carry):
        code = order_ref[5, r]
        slot = jnp.where(code < LANES, code, order_ref[4, jnp.maximum(code - LANES, 0)])
        pltpu.make_async_copy(blocks_ref.at[slot], out_ref.at[r], sem).start()
        return carry

    lax.fori_loop(0, LANES, move, 0)
    pltpu.make_async_copy(blocks_ref, out_ref, sem).wait()


def settle(order, blocks):
    return pl.pallas_call(
        settle_kernel,
        out_shape=jax.ShapeDtypeStruct(blocks.shape, blocks.dtype),
        in_specs=[pl.BlockSpec(memory_space=pltpu.SMEM), pl.BlockSpec(memory_space=pltpu.VMEM)],
        out_specs=pl.BlockSpec(memory_space=pl.ANY),
        scratch_shapes=[pltpu.SemaphoreType.DMA],
        name="settle",
    )(order, blocks)


def body(view_tokens, destinations, w_query, w_key, w_value, rate_vector, fast_gate, fast_up, fast_down, out_gain):
    width = view_tokens.shape[2]
    slots, order = scene(
        view_tokens.reshape(LANES, BLK, width), destinations, w_query, w_key, w_value, rate_vector,
        fast_gate, fast_up, fast_down, out_gain
    )
    out = settle(order, slots.reshape(LANES, BLK, width))
    return out.reshape(1, LANES * BLK, width)


def solution(mesh):
    placed = (P("lane", "ctx", None), P("lane", "ctx"), P(), P(), P(), P(), P(), P(), P(), P())
    return jax.shard_map(
        body, mesh=mesh, in_specs=placed, out_specs=P("lane", "ctx", None), check_vma=False
    )
```

```python
import jax
import jax.numpy as jnp
from jax import lax
from jax.experimental import pallas as pl
from jax.experimental.pallas import tpu as pltpu
from jax.sharding import PartitionSpec as P

MESH = pl.DeviceIdType.MESH
LANES = 64
BLK = 16
SIDE = 4
GROUPS = 4
ORDERS = ((2, 1, 0), (0, 2, 1), (1, 0, 2))


def coords_of(lane):
    return (lane // 16, (lane // 4) % 4, lane % 4)


def lane_of(coords):
    return coords[0] * 16 + coords[1] * 4 + coords[2]


def dot_nn(left, right):
    return jnp.dot(left, right, preferred_element_type=jnp.float32)


def dot_nt(left, right):
    return lax.dot_general(left, right, (((1,), (1,)), ((), ())), preferred_element_type=jnp.float32)


def row_scale(values):
    return lax.rsqrt(jnp.mean(values * values, axis=-1, keepdims=True) + 1e-06)


def offset_of(k):
    dz, dy = (k // 4) % SIDE, k % SIDE
    return dz, dy, (k // 16 + 2 * SIDE - dz - dy) % SIDE


def spread(row):
    return jnp.broadcast_to(row, (128, 128)).T[:LANES]


def prefix(counts, source):
    upto = counts
    shift = 1
    while shift < LANES:
        upto = upto + jnp.where(source >= shift, pltpu.roll(upto, shift, axis=0), 0)
        shift *= 2
    return upto - counts


def send_rows(dest_row):
    block = lax.broadcasted_iota(jnp.int32, (LANES, 128), 0)
    lane = lax.broadcasted_iota(jnp.int32, (LANES, 128), 1)
    lane_row = lax.broadcasted_iota(jnp.int32, (1, 128), 1)
    named = spread(dest_row) == lane
    count = jnp.sum(named.astype(jnp.int32), axis=0, keepdims=True)
    total = jnp.sum(jnp.where(named, block, 0), axis=0, keepdims=True)
    first = jnp.min(jnp.where(named, block, LANES - 1), axis=0, keepdims=True)

    def of(mask, value):
        return jnp.sum(spread(jnp.where(mask, value, 0)), axis=0, keepdims=True)

    twice = count == 2
    absent = (count == 0) & (lane_row < LANES)
    return first, of(twice, total - first), of(twice, lane_row), of(absent, lane_row)


def order_rows(doubled, missed, me):
    source = lax.broadcasted_iota(jnp.int32, (LANES, 128), 0)
    spot = lax.broadcasted_iota(jnp.int32, (LANES, 128), 1)
    usual = (missed != me).astype(jnp.int32)
    hole = 1 - usual
    double = (doubled == me).astype(jnp.int32)
    start = prefix(usual + double, source)
    hole_rank = prefix(hole, source)
    double_rank = prefix(double, source)
    dz, dy, dx = (me // 16 - source // 16) % SIDE, (me // 4 - source // 4) % SIDE, (me - source) % SIDE
    slot = ((dz + dy + dx) % SIDE) * 16 + dz * 4 + dy

    def row(mask, value):
        return jnp.sum(jnp.where(mask, value, 0), axis=0, keepdims=True)

    by_source = row(source == spot, hole_rank)
    filler = (double == 1) & (double_rank == by_source)
    return (
        row(source == spot, usual),
        row(filler, source // 16),
        row(filler, (source // 4) % SIDE),
        row(filler, source % SIDE),
        row((hole == 1) & (hole_rank == spot), slot),
        row((usual == 1) & (start == spot), slot)
        + row((double == 1) & (start + usual == spot), double_rank + LANES),
    )


def scene_kernel(view_hbm, dest_hbm, wq_hbm, wk_hbm, wv_hbm, rate_hbm, gate_hbm, up_hbm, down_hbm, gain_hbm,
                 out_ref, order_ref,
                 view, dest, wq, wk, wv, rate_row, gate, up, down, gain, rate_w,
                 idx_v, idx_s, rows_v, rows_s, send, prim, ext, metas,
                 tokens, queries, keys, values, term, hidden, asked, grad, grad_down, gu_w, down_w,
                 other_gu, other_down, sums, other_sums, result,
                 load_sem, local_sem, send_sem, recv_sem, ext_send, ext_recv, meta_send, meta_recv,
                 key_send, key_recv, val_send, val_recv, sum_send, sum_recv, w_send, w_recv):
    me = lax.axis_index("lane")
    ctx = lax.axis_index("ctx")
    here = coords_of(me)
    mate = (me, 1 - ctx)
    width = tokens.shape[1]
    half = width // 2
    part = width // 3
    chunk = tokens.shape[0] // GROUPS
    blocks = chunk // BLK
    step_size = 0.5 * width ** (-0.5)

    barrier = pltpu.get_barrier_semaphore()

    def greet(k, carry):
        pl.semaphore_signal(barrier, inc=1, device_id=(lax.rem(me + k, LANES), ctx), device_id_type=MESH)
        return carry

    lax.fori_loop(1, LANES, greet, 0)
    pl.semaphore_signal(barrier, inc=1, device_id=mate, device_id_type=MESH)

    loads = [
        pltpu.make_async_copy(a, b, load_sem.at[i])
        for i, (a, b) in enumerate((
            (dest_hbm, dest), (view_hbm, view), (wk_hbm, wk), (wv_hbm, wv), (wq_hbm, wq), (gate_hbm, gate),
            (up_hbm, up), (down_hbm, down), (rate_hbm, rate_row), (gain_hbm, gain)))
    ]
    for copy in loads:
        copy.start()
    loads[0].wait()

    first, second, doubled, missed = send_rows(jnp.concatenate([dest[...], dest[...]], axis=1))
    idx_v[0:1, :] = first
    idx_v[1:2, :] = second
    metas[here[0], here[1], here[2], 0:1, :] = doubled
    metas[here[0], here[1], here[2], 1:2, :] = missed
    to_idx = pltpu.make_async_copy(idx_v, idx_s, local_sem.at[0])
    to_idx.start()
    to_idx.wait()
    loads[1].wait()

    def block_of(b):
        return view[b]

    def peer(k):
        d = offset_of(k)
        return lane_of([(h + o) % SIDE for h, o in zip(here, d)])

    ext[here[0], here[1], here[2]] = block_of(idx_s[1, 0])
    prim[0] = block_of(idx_s[0, me])

    def pack(k, carry):
        send[k] = block_of(idx_s[0, peer(k)])
        return carry

    lax.fori_loop(1, LANES, pack, 0)
    pl.semaphore_wait(barrier, LANES)

    def stage_copy(ref, tail, order, stage, delta, back, sends, recvs):
        axis = order[stage]
        spot = list(here)
        if back:
            spot[axis] = (here[axis] - delta) % SIDE
        for done in order[:stage]:
            spot[done] = pl.ds(0, SIDE)
        to = list(here)
        to[axis] = (here[axis] + delta) % SIDE
        slab = ref.at[(*spot, *tail)]
        return pltpu.make_async_remote_copy(
            src_ref=slab, dst_ref=slab, send_sem=sends, recv_sem=recvs,
            device_id=(lane_of(to), ctx), device_id_type=MESH)

    def stage_copies(stage, back):
        made = []
        for delta in (1, 3, 2):
            made.append(stage_copy(
                metas, (), ORDERS[0], stage, delta, back,
                meta_send.at[stage, delta - 1], meta_recv.at[stage, delta - 1]))
            for p in range(3):
                made.append(stage_copy(
                    ext, (slice(None), pl.ds(p * part, part)), ORDERS[p], stage, delta, back,
                    ext_send.at[p, stage, delta - 1], ext_recv.at[p, stage, delta - 1]))
        return made

    def start_stage(stage):
        for copy in stage_copies(stage, False):
            copy.start()

    def end_stage(stage):
        for copy in stage_copies(stage, True):
            copy.wait_recv()

    def post(k, carry):
        pltpu.make_async_remote_copy(
            src_ref=send.at[k], dst_ref=prim.at[k],
            send_sem=send_sem, recv_sem=recv_sem.at[k // blocks],
            device_id=(peer(k), ctx), device_id_type=MESH).start()
        return carry

    start_stage(0)
    lax.fori_loop(1, blocks, post, 0)
    end_stage(0)
    start_stage(1)
    end_stage(1)
    start_stage(2)
    for copy in loads[2:]:
        copy.wait()
    mine = pl.ds(pl.multiple_of(ctx * half, 128), half)
    gu_w[0, pl.ds(0, half), :] = gate[:, mine].T
    gu_w[0, pl.ds(half, half), :] = up[:, mine].T
    down_w[0] = down[mine, :]
    rate_w[...] = jnp.broadcast_to(rate_row[...].astype(jnp.float32).reshape(1, width), (128, width)).T.astype(jnp.bfloat16)
    end_stage(2)
    lax.fori_loop(blocks, LANES, post, 0)
    table = metas[...].reshape(LANES, 2, 128)
    for i, row in enumerate(order_rows(table[:, 0, :], table[:, 1, :], me)):
        rows_v[i:i + 1, :] = row
    to_rows = pltpu.make_async_copy(rows_v, rows_s, local_sem.at[0])
    to_rows.start()
    to_order = pltpu.make_async_copy(rows_v, order_ref, local_sem.at[1])
    to_order.start()
    to_rows.wait()

    def share(ref, sends, recvs, seg, c):
        piece = ref.at[seg, pl.ds(c * chunk, chunk)]
        return pltpu.make_async_remote_copy(
            src_ref=piece, dst_ref=piece, send_sem=sends.at[c], recv_sem=recvs.at[c],
            device_id=mate, device_id_type=MESH)

    def fill(k, carry):
        d = offset_of(k)
        s = lane_of([(h - o) % SIDE for h, o in zip(here, d)])
        keep = rows_s[0, s].astype(jnp.float32)
        doubled_block = ext[rows_s[1, s], rows_s[2, s], rows_s[3, s]].astype(jnp.float32)
        block = prim[k].astype(jnp.float32) * keep + doubled_block * (1.0 - keep)
        tokens[pl.ds(pl.multiple_of(k * BLK, BLK), BLK), :] = block.astype(jnp.bfloat16)
        return carry

    def landed(lo, count, g):
        piece = prim.at[pl.ds(lo, count)]
        pltpu.make_async_remote_copy(
            src_ref=piece, dst_ref=piece, send_sem=send_sem, recv_sem=recv_sem.at[g],
            device_id=mate, device_id_type=MESH).wait_recv()

    def from_mate(c):
        share(keys, key_send, key_recv, 1 - ctx, c).wait_recv()
        share(values, val_send, val_recv, 1 - ctx, c).wait_recv()

    def terms(seg, c):
        rows = pl.ds(pl.multiple_of(c * chunk, chunk), chunk)
        pre = dot_nt(gu_w[seg], keys[seg, rows, :])
        back = dot_nt(down_w[seg], values[seg, rows, :])
        gate_pre, up_pre = pre[:half], pre[half:]
        gate_sig = jax.nn.sigmoid(gate_pre)
        gated = gate_pre * gate_sig
        hidden[:, rows] = (gated * up_pre).astype(jnp.bfloat16)
        term[pl.ds(0, half), rows] = (
            back * up_pre * gate_sig * (1.0 + gate_pre * (1.0 - gate_sig))
        ).astype(jnp.bfloat16)
        term[pl.ds(half, half), rows] = (back * gated).astype(jnp.bfloat16)

    def first_terms(c):
        @pl.when(ctx == 1)
        def _():
            from_mate(c)

        terms(0, c)

    def project(c, carry):
        @pl.when(c == 0)
        def _():
            landed(1, blocks - 1, 0)

        @pl.when(c > 0)
        def _():
            landed(c * blocks, blocks, c)

        lax.fori_loop(0, blocks, lambda j, carry: fill(c * blocks + j, carry), 0, unroll=16)
        rows = pl.ds(c * chunk, chunk)
        x = tokens[rows, :]
        k = dot_nn(x, wk[...])
        keys[ctx, rows, :] = (k * row_scale(k)).astype(jnp.bfloat16)
        share(keys, key_send, key_recv, ctx, c).start()
        rate = dot_nn(x, rate_w[...])
        rate = jnp.maximum(rate, 0.0) + jnp.log1p(jnp.exp(-jnp.abs(rate)))
        v = dot_nn(x, wv[...])
        values[ctx, rows, :] = (rate[:, :1] * v).astype(jnp.bfloat16)
        share(values, val_send, val_recv, ctx, c).start()
        q = dot_nn(x, wq[...])
        queries[rows, :] = (q * row_scale(q)).astype(jnp.bfloat16)

        @pl.when(c > 0)
        def _():
            first_terms(c - 1)

        return carry

    lax.fori_loop(0, GROUPS, project, 0)
    first_terms(GROUPS - 1)

    def share_sums(seg):
        return pltpu.make_async_remote_copy(
            src_ref=sums.at[seg], dst_ref=other_sums.at[seg], send_sem=sum_send.at[seg], recv_sem=sum_recv.at[seg],
            device_id=mate, device_id_type=MESH)

    def share_weights(seg, which=(0, 1, 2)):
        made = []
        for i in which:
            rows = pl.ds(i * half, half)
            source, target = (
                (down_w.at[seg + 1], other_down) if i == 2 else (gu_w.at[seg + 1, rows], other_gu.at[rows]))
            made.append(pltpu.make_async_remote_copy(
                src_ref=source, dst_ref=target, send_sem=w_send.at[i], recv_sem=w_recv.at[i],
                device_id=mate, device_id_type=MESH))
        return made

    def send_weights(seg, i):
        @pl.when(ctx == 1 - seg)
        def _():
            share_weights(seg, (i,))[0].start()

    def renew(seg):
        def slopes(j, carry):
            units = pl.ds(pl.multiple_of(j * half, 128), half)
            g = dot_nn(term[units, :], keys[seg])
            grad[units, :] = g
            sums[seg, pl.ds(j, 1), :] = jnp.sum(g * g, axis=0, keepdims=True)
            return carry

        lax.fori_loop(0, 2, slopes, 0)
        share_sums(seg).start()
        grad_down[...] = dot_nn(hidden[...], values[seg])
        g = grad_down[...]
        down_w[seg + 1] = (
            down_w[seg].astype(jnp.float32) + step_size * g * row_scale(g)
        ).astype(jnp.bfloat16)
        send_weights(seg, 2)
        share_sums(seg).wait_recv()
        for j in range(2):
            rows = pl.ds(j * half, half)
            total = sums[seg, pl.ds(j, 1), :] + other_sums[seg, pl.ds(j, 1), :]
            scale = step_size * lax.rsqrt(total * (1.0 / width) + 1e-06)
            gu_w[seg + 1, rows, :] = (
                gu_w[seg, rows, :].astype(jnp.float32) + grad[rows, :] * scale
            ).astype(jnp.bfloat16)
            send_weights(seg, j)

    renew(0)

    @pl.when(ctx == 0)
    def _():
        def one(c, carry):
            from_mate(c)
            return carry

        lax.fori_loop(0, GROUPS, one, 0)

    def second_terms(c, carry):
        terms(1, 2 * c)
        terms(1, 2 * c + 1)
        return carry

    lax.fori_loop(0, GROUPS // 2, second_terms, 0)
    renew(1)

    def answer_half(rows, gu):
        pre = dot_nt(queries[rows, :], gu)
        q_gate, q_up = pre[:, :half], pre[:, half:]
        return (q_gate * jax.nn.sigmoid(q_gate) * q_up).astype(jnp.bfloat16)

    def answer_own(c, carry):
        for i in range(2):
            rows = pl.ds((2 * c + i) * chunk, chunk)
            asked[rows, :] = answer_half(rows, gu_w[ctx + 1])
        return carry

    lax.fori_loop(0, GROUPS // 2, answer_own, 0)
    for copy in share_weights(0):
        copy.wait_recv()

    def out_copy(c):
        rows = pl.ds(c * chunk, chunk)
        return pltpu.make_async_copy(result.at[rows], out_ref.at[rows], load_sem.at[c])

    def answer_one(c):
        rows = pl.ds(c * chunk, chunk)
        y = dot_nn(asked[rows, :], down_w[ctx + 1])
        y = y + dot_nn(answer_half(rows, other_gu[...]), other_down[...])
        result[rows, :] = (y * row_scale(y) * gain[...].reshape(1, width)).astype(jnp.bfloat16)
        out_copy(c).start()

    def answer(c, carry):
        answer_one(2 * c)
        answer_one(2 * c + 1)
        return carry

    lax.fori_loop(0, GROUPS // 2, answer, 0)

    def sent(c, carry):
        share(keys, key_send, key_recv, ctx, c).wait_send()
        share(values, val_send, val_recv, ctx, c).wait_send()
        out_copy(c).wait()
        return carry

    lax.fori_loop(0, GROUPS, sent, 0)
    for seg in range(2):
        share_sums(seg).wait_send()
    for copy in share_weights(0):
        copy.wait_send()
    for stage in range(3):
        for copy in stage_copies(stage, False):
            copy.wait_send()
    to_order.wait()
    piece = send.at[pl.ds(1, LANES - 1)]
    pltpu.make_async_remote_copy(
        src_ref=piece, dst_ref=piece, send_sem=send_sem, recv_sem=recv_sem.at[0],
        device_id=mate, device_id_type=MESH).wait_send()


def scene(*operands):
    width = operands[0].shape[2]
    rows = LANES * BLK
    half = width // 2
    any_ = pl.BlockSpec(memory_space=pl.ANY)
    bf, f32, i32, dma, vmem = jnp.bfloat16, jnp.float32, jnp.int32, pltpu.SemaphoreType.DMA, pltpu.VMEM
    square = vmem((width, width), bf)
    return pl.pallas_call(
        scene_kernel,
        out_shape=(jax.ShapeDtypeStruct((rows, width), bf), jax.ShapeDtypeStruct((8, 128), i32)),
        in_specs=[any_] * len(operands),
        out_specs=(any_, any_),
        scratch_shapes=[
            vmem((LANES, BLK, width), bf), vmem((1, LANES), i32), square, square, square, vmem((width,), bf),
            square, square, square, vmem((width,), f32), vmem((width, 128), bf),
            vmem((8, 128), i32), pltpu.SMEM((8, 128), i32), vmem((8, 128), i32), pltpu.SMEM((8, 128), i32),
            vmem((LANES, BLK, width), bf), vmem((LANES, BLK, width), bf),
            vmem((SIDE, SIDE, SIDE, BLK, width), bf), vmem((SIDE, SIDE, SIDE, 2, 128), i32),
            vmem((rows, width), bf), vmem((rows, width), bf),
            vmem((2, rows, width), bf), vmem((2, rows, width), bf), vmem((width, rows), bf), vmem((half, rows), bf),
            vmem((rows, half), bf),
            vmem((width, width), f32), vmem((half, width), f32),
            vmem((3, width, width), bf), vmem((3, half, width), bf),
            square, vmem((half, width), bf), vmem((2, 8, width), f32), vmem((2, 8, width), f32), vmem((rows, width), bf),
            dma((10,)), dma((2,)), dma, dma((GROUPS,)),
            dma((3, 3, 3)), dma((3, 3, 3)), dma((3, 3)), dma((3, 3)),
            dma((4,)), dma((4,)), dma((4,)), dma((4,)), dma((2,)), dma((2,)), dma((3,)), dma((3,)),
        ],
        compiler_params=pltpu.CompilerParams(
            collective_id=0, has_side_effects=True, vmem_limit_bytes=60 << 20
        ),
        name="scene",
    )(*operands)


def settle_kernel(order_ref, blocks_ref, out_ref, sem):
    def move(r, carry):
        code = order_ref[5, r]
        slot = jnp.where(code < LANES, code, order_ref[4, jnp.maximum(code - LANES, 0)])
        pltpu.make_async_copy(blocks_ref.at[slot], out_ref.at[r], sem).start()
        return carry

    lax.fori_loop(0, LANES, move, 0)
    pltpu.make_async_copy(blocks_ref, out_ref, sem).wait()


def settle(order, blocks):
    return pl.pallas_call(
        settle_kernel,
        out_shape=jax.ShapeDtypeStruct(blocks.shape, blocks.dtype),
        in_specs=[pl.BlockSpec(memory_space=pltpu.SMEM), pl.BlockSpec(memory_space=pltpu.VMEM)],
        out_specs=pl.BlockSpec(memory_space=pl.ANY),
        scratch_shapes=[pltpu.SemaphoreType.DMA],
        name="settle",
    )(order, blocks)


def body(view_tokens, destinations, w_query, w_key, w_value, rate_vector, fast_gate, fast_up, fast_down, out_gain):
    width = view_tokens.shape[2]
    slots, order = scene(
        view_tokens.reshape(LANES, BLK, width), destinations, w_query, w_key, w_value, rate_vector,
        fast_gate, fast_up, fast_down, out_gain
    )
    out = settle(order, slots.reshape(LANES, BLK, width))
    return out.reshape(1, LANES * BLK, width)


def solution(mesh):
    placed = (P("lane", "ctx", None), P("lane", "ctx"), P(), P(), P(), P(), P(), P(), P(), P())
    return jax.shard_map(
        body, mesh=mesh, in_specs=placed, out_specs=P("lane", "ctx", None), check_vma=False
    )
```
